32 devices in a mesh: groups: 2 (over x), rows: 16 (over z, y, core).
Axes of the slice: x: 2, y: 2, z: 4, core: 2. Of those that a mesh axis runs over, the one named last changes fastest.
Arguments:
- volume: bfloat16 [32, 128, 8, 512], P(None, ('groups', 'rows')), parts along dimension 1, may hold values from -6 to 6
- fine_first: bfloat16 [3, 3, 3, 32, 32], replicated, may hold values from -0.3125 to 0.3125
- fine_second: bfloat16 [3, 3, 3, 32, 32], replicated, may hold values from -0.3125 to 0.3125
- middle_first: bfloat16 [3, 3, 3, 64, 32], replicated, may hold values from -0.3125 to 0.3125
- middle_second: bfloat16 [3, 3, 3, 64, 64], replicated, may hold values from -0.21875 to 0.21875
- bottom_first: bfloat16 [3, 3, 3, 256, 64], P(None, None, None, 'rows'), may hold values from -0.21875 to 0.21875
- bottom_second: bfloat16 [3, 3, 3, 256, 256], P(None, None, None, 'rows'), may hold values from -0.109375 to 0.109375
- upsample_bottom: bfloat16 [2, 2, 2, 64, 256], replicated, may hold values from -1.5 to 1.5
- middle_merge: bfloat16 [3, 3, 3, 64, 128], replicated, may hold values from -0.078125 to 0.078125
- middle_refine: bfloat16 [3, 3, 3, 64, 64], replicated, may hold values from -0.21875 to 0.21875
- upsample_middle: bfloat16 [2, 2, 2, 32, 64], replicated, may hold values from -1.5 to 1.5
- fine_merge: bfloat16 [3, 3, 3, 32, 64], replicated, may hold values from -0.109375 to 0.109375
- fine_refine: bfloat16 [3, 3, 3, 32, 32], replicated, may hold values from -0.3125 to 0.3125
Outputs:
- decoded: bfloat16 [32, 128, 8, 512], P(None, ('groups', 'rows')), parts along dimension 1
The draws below stay inside these ranges and needn't reach their ends.
There are 2 independent parts, one for each index of `groups`. The reference program is written for one: setup_inputs(seed, part) draws one part's arguments, and reference() takes and returns one part's arrays. A program takes and returns all parts, laid end to end along the dimension named above; an argument that names none is the same for every part. Nothing has to cross between parts.
All inputs are finite; a program needn't handle non-finite values.
Results may differ from the reference program's by a relative error of at most 0.02.
Values may be sent and summed in bfloat16 or wider, within the bound.
A program may use at most 128 MiB of HBM per device.

```python
import jax
import jax.numpy as jnp
from jax import lax

C1 = 32
C2 = 64
C3 = 256
DEPTH = 8
WIDTH = 512
HEIGHT = 64


def block_levels(rng, dims, cuts, smallest, high):
    def one(axis_at, blocks):
        draws = jax.random.uniform(jax.random.fold_in(jax.random.fold_in(rng, 6), axis_at), (blocks,), jnp.float32, smallest / len(cuts), high / len(cuts))
        return jnp.repeat(jnp.exp(draws), dims[axis_at] // blocks).reshape((-1,) + (1,) * (len(dims) - axis_at - 1))

    loudness = one(*cuts[0])
    for cut in cuts[1:]:
        loudness = loudness * one(*cut)
    return loudness


def bell_draw(own_key, dims, scale, limit, split=(), held_as=jnp.bfloat16):
    array = scale * jax.random.normal(own_key, dims, jnp.float32)
    if split:
        array = array * block_levels(own_key, dims, split, -0.22, 0.18)
    return jnp.clip(array, -limit, limit).astype(held_as)


def setup_inputs(seed: int = 0, part: int = 0) -> dict:
    seeds = jax.random.split(jax.random.key(seed), 14)
    own_keys = jax.random.split(jax.random.fold_in(seeds[13], part), 14)
    volume = bell_draw(own_keys[0], (C1, HEIGHT, DEPTH, WIDTH), 1.0, 6.0, ((1, 16),))
    fine_first = bell_draw(seeds[1], (3, 3, 3, C1, C1), (27 * C1 // 2) ** -0.5, 0.3125)
    fine_second = bell_draw(seeds[2], (3, 3, 3, C1, C1), (27 * C1 // 2) ** -0.5, 0.3125)
    middle_first = bell_draw(seeds[3], (3, 3, 3, C2, C1), (27 * C1 // 2) ** -0.5, 0.3125)
    middle_second = bell_draw(seeds[4], (3, 3, 3, C2, C2), (27 * C2 // 2) ** -0.5, 0.21875)
    bottom_first = bell_draw(seeds[5], (3, 3, 3, C3, C2), (27 * C2 // 2) ** -0.5, 0.21875, ((3, 16),))
    bottom_second = bell_draw(seeds[6], (3, 3, 3, C3, C3), (27 * C3 // 2) ** -0.5, 0.109375, ((3, 16),))
    upsample_bottom = bell_draw(seeds[7], (2, 2, 2, C2, C3), (C3 // 16) ** -0.5, 1.5)
    middle_merge = bell_draw(seeds[8], (3, 3, 3, C2, 2 * C2), (108 * C2) ** -0.5, 0.078125)
    middle_refine = bell_draw(seeds[9], (3, 3, 3, C2, C2), (27 * C2 // 2) ** -0.5, 0.21875)
    upsample_middle = bell_draw(seeds[10], (2, 2, 2, C1, C2), (C2 // 4) ** -0.5, 1.5)
    fine_merge = bell_draw(seeds[11], (3, 3, 3, C1, 2 * C1), (108 * C1) ** -0.5, 0.109375)
    fine_refine = bell_draw(seeds[12], (3, 3, 3, C1, C1), (27 * C1 // 2) ** -0.5, 0.3125)
    return {"volume": volume, "fine_first": fine_first, "fine_second": fine_second, "middle_first": middle_first, "middle_second": middle_second, "bottom_first": bottom_first, "bottom_second": bottom_second, "upsample_bottom": upsample_bottom, "middle_merge": middle_merge, "middle_refine": middle_refine, "upsample_middle": upsample_middle, "fine_merge": fine_merge, "fine_refine": fine_refine}


leakage = 0.01


def conv_layer(features, kernel):
    result = lax.conv_general_dilated(features[None].astype(jnp.float32), kernel.astype(jnp.float32), (1, 1, 1), ((1, 1), (1, 1), (1, 1)), dimension_numbers=("NCDHW", "DHWOI", "NCDHW"), precision=lax.Precision.HIGHEST)
    return jax.nn.leaky_relu(result[0], leakage).astype(jnp.bfloat16)


def max_pool(features):
    chans, height, depth, width = features.shape
    return features.reshape(chans, height // 2, 2, depth // 2, 2, width // 2, 2).max(axis=(2, 4, 6))


def up_sample(features, kernel):
    chans, height, depth, width = features.shape
    result = jnp.einsum("abcoi,ihzw->ohazbwc", kernel.astype(jnp.float32), features.astype(jnp.float32), precision=lax.Precision.HIGHEST)
    return result.reshape(kernel.shape[3], 2 * height, 2 * depth, 2 * width).astype(jnp.bfloat16)


def reference(volume, fine_first, fine_second, middle_first, middle_second, bottom_first, bottom_second, upsample_bottom, middle_merge, middle_refine, upsample_middle, fine_merge, fine_refine):
    fine_one = conv_layer(volume, fine_first)
    fine_two = conv_layer(fine_one, fine_second)
    middle_one = conv_layer(max_pool(fine_two), middle_first)
    middle_two = conv_layer(middle_one, middle_second)
    bottom_one = conv_layer(max_pool(middle_two), bottom_first)
    bottom_two = conv_layer(bottom_one, bottom_second)
    lifted = up_sample(bottom_two, upsample_bottom)
    middle_three = conv_layer(jnp.concatenate([middle_two, lifted], axis=0), middle_merge)
    middle_four = conv_layer(middle_three, middle_refine)
    raised = up_sample(middle_four, upsample_middle)
    fine_three = conv_layer(jnp.concatenate([fine_two, raised], axis=0), fine_merge)
    return conv_layer(fine_three, fine_refine)
```

```python
import functools

import jax
import jax.numpy as jnp
from jax import lax
from jax.experimental import pallas as pl
from jax.experimental.pallas import tpu as pltpu
from jax.sharding import PartitionSpec as P

leakage = 0.01
bf16, f32 = jnp.bfloat16, jnp.float32
VMEM_LIMIT = 56 * 2**20


def iota(shape, axis):
    return lax.broadcasted_iota(jnp.int32, shape, axis)


def one_hot(mask):
    return jnp.where(mask, 1.0, 0.0).astype(bf16)


def dot(a, b):
    return jnp.dot(a, b, preferred_element_type=f32)


def spread(total, channels, offset, copies):
    shape = (total, copies * channels)
    return one_hot((iota(shape, 1) & (channels - 1)) + offset == iota(shape, 0))


def band(target, tap, outs, ins, depth):
    block = iota((outs, depth * ins), 1) // ins
    zero = jnp.zeros((outs, depth * ins), f32)
    for a in range(3):
        for c in range(3):
            taps = [tap(a, b, c) for b in range(3)]
            for z in range(depth):
                rows = zero
                for b in range(3):
                    if 0 <= z + b - 1 < depth:
                        rows = jnp.where(block == z + b - 1, taps[b], rows)
                start = (c * depth + z) * outs
                target[start : start + outs, a * depth * ins : (a + 1) * depth * ins] = rows.astype(bf16)


def band_kernel(target, kernel_ref, outs, total, ins, offset, depth, turned=False):
    picks = spread(total, ins, offset, depth)

    def tap(a, b, c):
        at = (a * 3 + b) * 3 + c
        if turned:
            block = kernel_ref[at * total : (at + 1) * total, :]
            return lax.dot_general(block, picks, (((0,), (0,)), ((), ())), preferred_element_type=f32)
        return dot(kernel_ref[at * outs : (at + 1) * outs, :], picks)

    band(target, tap, outs, ins, depth)


def finish(sums, count, period):
    width = sums.shape[1]
    lane = iota((count, width), 1) & (period - 1)
    left = jnp.where(lane == 0, 0.0, pltpu.roll(sums[:count], 1, 1))
    right = jnp.where(lane == period - 1, 0.0, pltpu.roll(sums[2 * count :], width - 1, 1))
    total = left + sums[count : 2 * count] + right
    return jnp.maximum(total, leakage * total).astype(bf16)


def conv_row(sources, at, count):
    sums = None
    for banded, rows, cells in sources:
        window = rows[pl.ds(pl.multiple_of(at * cells, cells), 3 * cells), :]
        part = dot(banded[...], window)
        sums = part if sums is None else sums + part
    return finish(sums, count, sums.shape[1])


def conv_rows(sources, target, cells, first, step, number, shift):
    def one(at):
        to = pl.multiple_of((at + shift) * cells, cells)
        target[pl.ds(to, cells), :] = conv_row(sources, at, cells)

    if number == 1:
        one(first)
    else:

        @pl.loop(0, number)
        def _(index):
            one(first + index * step)


class Halo:
    def __init__(self, edges, at, buf, cells, source, target, number, step):
        self.edges, self.buf, self.step = edges, buf, step
        self.source = pl.ds(source * cells, number * cells)
        self.target = pl.ds(target * cells, number * cells)
        self.gives, self.takes = edges.has(step), edges.has(-step)
        self.at = at

    def copy(self):
        return pltpu.make_async_remote_copy(
            src_ref=self.buf.at[self.source],
            dst_ref=self.buf.at[self.target],
            send_sem=self.edges.send.at[self.at],
            recv_sem=self.edges.recv.at[self.at],
            device_id=(self.edges.group, self.edges.me + self.step),
            device_id_type=pl.DeviceIdType.MESH,
        )

    def start(self):
        @pl.when(self.gives)
        def _():
            self.copy().start()

    def arrive(self):
        @pl.when(self.takes)
        def _():
            self.copy().wait_recv()

        @pl.when(jnp.logical_not(self.takes))
        def _():
            self.buf[self.target, :] = jnp.zeros((self.target.size, self.buf.shape[1]), bf16)

    def sent(self):
        @pl.when(self.gives)
        def _():
            self.copy().wait_send()


class Edges:
    def __init__(self, groups, rows, count, send, recv):
        self.group, self.me, self.count = lax.axis_index(groups), lax.axis_index(rows), count
        self.send, self.recv = send, recv
        self.halos = []

    def has(self, step):
        other = self.me + step
        return (other >= 0) & (other < self.count)

    def greet(self, others, reach):
        barrier = pltpu.get_barrier_semaphore()

        def signal(to):
            pl.semaphore_signal(barrier, inc=1, device_id=(self.group, to), device_id_type=pl.DeviceIdType.MESH)

        for other in others:
            signal(other)
        number = len(others)
        for distance in range(1, reach + 1):
            for step in (-distance, distance):

                @pl.when(self.has(step))
                def _():
                    signal(self.me + step)

                number = number + jnp.where(self.has(step), 1, 0)
        pl.semaphore_wait(barrier, number)

    def pair(self, buf, cells, own, height, number):
        up = Halo(self, len(self.halos), buf, cells, own, own + height, number, -1)
        self.halos.append(up)
        down = Halo(self, len(self.halos), buf, cells, own + height - number, own - number, number, 1)
        self.halos.append(down)
        return [up, down]

    def fan(self, buf, cells, own, reach):
        fans = []
        for distance in range(1, reach + 1):
            for step in (-distance, distance):
                fans.append(Halo(self, len(self.halos), buf, cells, own, own - step, 1, step))
                self.halos.append(fans[-1])
        return fans

    def blank(self, buf, cells, row, step):
        @pl.when(jnp.logical_not(self.has(step)))
        def _():
            buf[row * cells : (row + 1) * cells, :] = jnp.zeros((cells, buf.shape[1]), bf16)


def start(halos):
    for halo in halos:
        halo.start()


def arrive(halos):
    for halo in halos:
        halo.arrive()


class Ring:
    def __init__(self, edges, whole, send, recv, side_send, side_recv):
        self.edges, self.whole = edges, whole
        self.sems = send, recv, side_send, side_recv
        self.chips = edges.count // 2
        self.core = lax.rem(edges.me, 2)
        chip = edges.me // 2
        self.place = jnp.where(lax.rem(chip, 2) == 0, chip // 2, self.chips - 1 - chip // 2)
        self.mate = edges.me + 1 - 2 * self.core
        self.cut = whole.shape[1] // 2

    def at(self, place):
        place = lax.rem(place + 2 * self.chips, self.chips)
        chip = jnp.where(place < self.chips // 2, 2 * place, 2 * (self.chips - 1 - place) + 1)
        return 2 * chip + self.core

    def neighbours(self):
        return [self.at(self.place + 1), self.at(self.place - 1)]

    def copy(self, slot, way, to, send, recv):
        part = self.whole.at[slot, pl.ds(way * self.cut, self.cut)]
        return pltpu.make_async_remote_copy(
            src_ref=part,
            dst_ref=part,
            send_sem=send,
            recv_sem=recv,
            device_id=(self.edges.group, to),
            device_id_type=pl.DeviceIdType.MESH,
        )

    def hop(self, step, way):
        sign = 1 - 2 * way
        send, recv = self.sems[0].at[step, way], self.sems[1].at[step, way]
        return self.copy(self.at(self.place - sign * step), way, self.at(self.place + sign), send, recv)

    def landed(self, step, way):
        sign = 1 - 2 * way
        send, recv = self.sems[0].at[step, way], self.sems[1].at[step, way]
        return self.copy(self.at(self.place - sign * (step + 1)), way, self.at(self.place + sign), send, recv)

    def across(self, step, way, other=False):
        sign = 1 - 2 * way
        slot = self.at(self.place - sign * (step + 1))
        slot = slot + 1 - 2 * self.core if other else slot
        return self.copy(slot, way, self.mate, self.sems[2].at[step + 1, way], self.sems[3].at[step + 1, way])

    def step(self, at):
        if isinstance(at, int) and at >= self.chips:
            return
        for way in range(2):
            if not isinstance(at, int) or at > 0:
                self.landed(at - 1, way).wait_recv()
            if not isinstance(at, int) or at < self.chips - 1:
                self.hop(at, way).start()
            self.across(at - 1, way).start()

    def finish(self, done):
        if done < self.chips:

            @pl.loop(done, self.chips - 1)
            def _(at):
                self.step(at)

            self.step(self.chips - 1)

        @pl.loop(0, self.chips)
        def _(at):
            for way in range(2):
                self.across(at - 1, way, True).wait_recv()

    def sent(self):
        @pl.loop(0, self.chips)
        def _(at):
            for way in range(2):
                self.across(at - 1, way).wait_send()

        @pl.loop(0, self.chips - 1)
        def _(at):
            for way in range(2):
                self.hop(at, way).wait_send()


def halves(width):
    half = width // 2
    source, target = iota((width, width), 0), iota((width, width), 1)
    return one_hot(source == jnp.where(target < half, 2 * target, 2 * (target - half) + 1))


def weave(width):
    half = width // 2
    source, target = iota((width, width), 0), iota((width, width), 1)
    return one_hot(target == jnp.where(source < half, 2 * source, 2 * (source - half) + 1))


def pool(first, second, chans, parts):
    rows = jnp.maximum(first, second)
    depth, width = rows.shape[0] // chans, rows.shape[1]
    pairs = [
        jnp.maximum(rows[z * chans : (z + 1) * chans], rows[(z + 1) * chans : (z + 2) * chans])
        for z in range(0, depth, 2)
    ]
    split = dot(jnp.concatenate(pairs, axis=0), parts)
    return jnp.maximum(split[:, : width // 2], split[:, width // 2 :]).astype(bf16)


def lift(rows, kernel_ref, ins, outs, woven, store, which=(0, 1)):
    depth = rows.shape[0] // ins
    for a in which:
        kernel = kernel_ref[a * 4 * outs : (a + 1) * 4 * outs, :]
        parts = [dot(kernel, rows[z * ins : (z + 1) * ins]).astype(bf16) for z in range(depth)]
        stack = []
        for z in range(depth):
            for b in range(2):
                at = b * 2 * outs
                stack.append(jnp.concatenate([parts[z][at : at + outs], parts[z][at + outs : at + 2 * outs]], axis=1))
        store(a, dot(jnp.concatenate(stack, axis=0), woven).astype(bf16))


def network(size, groups, rows, count, *refs):
    (vol, b2, b1, k1, k2, k3, k4, ub, mm, mr, um, fm, fr, out) = refs[:14]
    (b_vol, b_one, b_pool, b_first, e1, e2, e3, e4) = refs[14:22]
    (b_fine, b_mid, b_low, b_bot, bot, b_lift, b_three, four, b_raise, b_last) = refs[22:32]
    (kt, t1, t2, t3a, t3b, t4, t5a, t5b, t6, whole) = refs[32:42]
    (send, recv, ring_send, ring_recv, side_send, side_recv, local) = refs[42:]
    H, Z, W, C1, C2, C3 = size
    R, R2, RP, RB = Z * C1, Z // 2 * C2, Z // 4 * C2, Z // 4 * C3
    RQ = Z // 2 * C1
    H2 = H // 2
    side = C3 // C2
    each = -(-27 // side)
    edges = Edges(groups, rows, count, send, recv)
    ring = Ring(edges, whole, ring_send, ring_recv, side_send, side_recv)
    vol_halo = edges.pair(b_vol, R, 1, H, 1)
    one_halo = edges.pair(b_one, R, 1, H, 1)
    pool_halo = edges.pair(b_pool, RQ, 2, H2, 2)
    low_halo = edges.fan(b_low, RP, 3, 3)
    mid_halo = edges.pair(b_mid, R2, 2, H2, 2)
    fine_halo = edges.pair(b_fine, R, 2, H, 2)
    four_halo = edges.pair(four, R2, 1, H2, 1)
    loads = [
        pltpu.make_async_copy(vol, b_vol.at[pl.ds(R, H * R)], local.at[0]),
        pltpu.make_async_copy(b2, whole.at[edges.me, pl.ds(0, 27)], local.at[1]),
    ]
    for load in loads:
        load.start()
    for t in range(each):
        taps = [b1[q * each + t] if q * each + t < 27 else jnp.zeros(b1.shape[1:], bf16) for q in range(side)]
        whole[edges.me, 27 + t] = jnp.concatenate(taps, axis=-1)
    edges.greet(ring.neighbours(), 3)
    loads[0].wait()
    start(vol_halo)
    loads[1].wait()
    ring.step(0)
    band_kernel(e1, k1, C1, C1, C1, 0, Z)
    conv_rows([(e1, b_vol, R)], b_one, R, 1, 1, H - 2, 1)
    band_kernel(e2, k2, C1, C1, C1, 0, Z)
    band_kernel(e3, k3, C2, C1, C1, 0, Z // 2, True)
    arrive(vol_halo)
    ring.step(1)
    conv_rows([(e1, b_vol, R)], b_one, R, 0, H - 1, 2, 1)
    start(one_halo)
    conv_rows([(e2, b_one, R)], b_fine, R, 1, 1, H - 2, 2)
    ring.step(2)
    band_kernel(e4, k4, C2, C2, C2, 0, Z // 2)
    band_kernel(t3a, mm, C2, 2 * C2, C2, 0, Z // 2)
    arrive(one_halo)
    ring.step(3)
    conv_rows([(e2, b_one, R)], b_fine, R, 0, H - 1, 2, 2)
    parts = halves(W)
    for h in range(H2):
        first, second = b_fine[(2 * h + 2) * R : (2 * h + 3) * R, :], b_fine[(2 * h + 3) * R : (2 * h + 4) * R, :]
        b_pool[(h + 2) * RQ : (h + 3) * RQ, :] = pool(first, second, C1, parts)
    start(pool_halo)
    ring.step(4)
    band_kernel(t3b, mm, C2, 2 * C2, C2, C2, Z // 2)
    band_kernel(t4, mr, C2, C2, C2, 0, Z // 2)
    band_kernel(t5a, fm, C1, 2 * C1, C1, 0, Z)
    band_kernel(t5b, fm, C1, 2 * C1, C1, C1, Z)
    band_kernel(t6, fr, C1, C1, C1, 0, Z)
    ring.step(5)
    arrive(pool_halo)
    conv_rows([(e3, b_pool, RQ)], b_first, R2, 0, 1, H2 + 2, 0)
    edges.blank(b_first, R2, 0, -1)
    edges.blank(b_first, R2, H2 + 1, 1)
    ring.step(6)
    conv_rows([(e4, b_first, R2)], b_mid, R2, 0, 1, H2, 2)
    first, second = b_mid[2 * R2 : 3 * R2, :], b_mid[3 * R2 : 4 * R2, :]
    b_low[3 * RP : 4 * RP, :] = pool(first, second, C2, halves(W // 2))
    start(low_halo)
    ring.finish(7)
    start(mid_halo)
    start(fine_halo)
    wide = Z // 4 * C2
    shape = (C3, side * wide)
    picks = one_hot(iota(shape, 0) == iota(shape, 1) // wide * C2 + (iota(shape, 1) & (C2 - 1)))
    for t in range(each):
        taps = dot(whole[:, 27 + t].reshape(C3, C3), picks).astype(bf16)
        for q in range(side):
            if q * each + t < 27:
                at = (q * each + t) * C3
                kt[at : at + C3, :] = taps[:, q * wide : (q + 1) * wide]

    def tap(a, b, c):
        at = ((a * 3 + b) * 3 + c) * C3
        return kt[at : at + C3, :].astype(f32)

    band(t1, tap, C3, C2, Z // 4)
    for a in range(3):
        for c in range(3):
            for z in range(Z // 4):
                for y in range(Z // 4):
                    r, l = (c * (Z // 4) + z) * C3, (a * (Z // 4) + y) * C3
                    if -1 <= y - z <= 1:
                        t2[r : r + C3, l : l + C3] = whole[:, (a * 3 + y - z + 1) * 3 + c].reshape(C3, C3)
                    else:
                        t2[r : r + C3, l : l + C3] = jnp.zeros((C3, C3), bf16)
    arrive(low_halo)
    narrow = W // 4

    def bottom(banded, source, cells, target, number):
        rows = jnp.concatenate([source[at * cells : (at + 3) * cells, :] for at in range(number)], axis=1)
        for z in range(Z // 4):
            sums = [dot(banded[(c * (Z // 4) + z) * C3 : (c * (Z // 4) + z + 1) * C3, :], rows) for c in range(3)]
            done = finish(jnp.concatenate(sums, axis=0), C3, narrow)
            for at in range(number):
                target[at * RB + z * C3 : at * RB + (z + 1) * C3, :] = done[:, at * narrow : (at + 1) * narrow]

    bottom(t1, b_low, RP, b_bot, 5)
    for step in (-2, -1, 1, 2):
        edges.blank(b_bot, RB, 2 + step, step)
    bottom(t2, b_bot, RB, bot, 3)
    for step in (-1, 1):
        edges.blank(bot, RB, 1 + step, step)
    woven = weave(W // 2)
    for h in range(3):

        def store(a, value):
            at = (2 * h + a) * R2
            b_lift[at : at + R2, :] = value

        lift(bot[h * RB : (h + 1) * RB, :], ub, C3, C2, woven, store)
    arrive(mid_halo)
    conv_rows([(t3a, b_mid, R2), (t3b, b_lift, R2)], b_three, R2, 0, 1, H2 + 2, 0)
    edges.blank(b_three, R2, 0, -1)
    edges.blank(b_three, R2, H2 + 1, 1)
    conv_rows([(t4, b_three, R2)], four, R2, 0, 1, H2, 1)
    start(four_halo)
    woven = weave(W)

    def raise_row(h, which=(0, 1)):
        def store(a, value):
            at = (2 * h + a) * R
            b_raise[at : at + R, :] = value

        lift(four[h * R2 : (h + 1) * R2, :], um, C2, C1, woven, store, which)

    for h in range(1, H2 + 1):
        raise_row(h)
    sources = [(t5a, b_fine, R), (t5b, b_raise, R)]
    conv_rows(sources, b_last, R, 2, 1, H - 2, 0)
    arrive(four_halo)
    arrive(fine_halo)
    raise_row(0)
    raise_row(H2 + 1)
    conv_rows(sources, b_last, R, 0, 1, 2, 0)
    conv_rows(sources, b_last, R, H, 1, 2, 0)
    edges.blank(b_last, R, 0, -1)
    edges.blank(b_last, R, H + 1, 1)
    conv_rows([(t6, b_last, R)], out, R, 0, 1, H, 0)
    for halo in edges.halos:
        halo.sent()
    ring.sent()


def per_device(count, *args):
    (volume, f1, f2, m1, m2, b1, b2, ub, mm, mr, um, fm, fr) = args
    C1, H, Z, W = volume.shape
    C2, C3 = m1.shape[3], b2.shape[4]
    own = b1.shape[3]
    R, R2, RP, RL, RB = Z * C1, Z // 2 * C2, Z // 2 * C1, Z // 4 * C2, Z // 4 * C3
    H2, W2, W4 = H // 2, W // 2, W // 4
    assert H == 4
    flat = lambda k: k.reshape(-1, k.shape[-1])
    each = -(-27 // (C3 // C2))
    taps = 27 + each + (27 + each) % 2
    chips = count // 2
    cells = volume.transpose(1, 2, 0, 3).reshape(H * R, W)
    vmem, hbm = pl.BlockSpec(memory_space=pltpu.VMEM), pl.BlockSpec(memory_space=pl.ANY)
    V = lambda *shape: pltpu.VMEM(shape, bf16)
    D = pltpu.SemaphoreType.DMA
    out = pl.pallas_call(
        functools.partial(network, (H, Z, W, C1, C2, C3), "groups", "rows", count),
        out_shape=jax.ShapeDtypeStruct((H * R, W), bf16),
        in_specs=[hbm] * 2 + [vmem] * 11,
        out_specs=vmem,
        scratch_shapes=[
            V((H + 2) * R, W), V((H + 2) * R, W), V((H2 + 4) * RP, W2), V((H2 + 2) * R2, W2),
            V(3 * R, 3 * R), V(3 * R, 3 * R), V(3 * R2, 3 * RP), V(3 * R2, 3 * R2),
            V((H + 4) * R, W), V((H2 + 4) * R2, W2), V(7 * RL, W4), V(5 * RB, W4), V(3 * RB, W4),
            V((H2 + 4) * R2, W2), V((H2 + 2) * R2, W2), V((H2 + 2) * R2, W2), V((H + 4) * R, W), V((H + 2) * R, W),
            V(27 * C3, Z // 4 * C2), V(3 * RB, 3 * RL), V(3 * RB, 3 * RB), V(3 * R2, 3 * R2), V(3 * R2, 3 * R2),
            V(3 * R2, 3 * R2), V(3 * R, 3 * R), V(3 * R, 3 * R), V(3 * R, 3 * R), V(count, taps, own, C3),
            D((18,)), D((18,)), D((chips - 1, 2)), D((chips - 1, 2)), D((chips, 2)), D((chips, 2)), D((2,)),
        ],
        compiler_params=pltpu.CompilerParams(collective_id=0, has_side_effects=True, vmem_limit_bytes=VMEM_LIMIT),
        name="network",
    )(
        cells, b2.reshape(27, own, C3), b1.reshape(27, own, C2), flat(f1), flat(f2), flat(m1.swapaxes(3, 4)), flat(m2),
        flat(ub), flat(mm), flat(mr), flat(um), flat(fm), flat(fr),
    )
    return out.reshape(H, Z, C1, W).transpose(2, 0, 1, 3)


def solution(mesh):
    placed = [P(None, ("groups", "rows"), None, None)] + [P()] * 12
    placed[5] = placed[6] = P(None, None, None, "rows", None)
    return jax.shard_map(
        functools.partial(per_device, mesh.shape["rows"]),
        mesh=mesh,
        in_specs=tuple(placed),
        out_specs=P(None, ("groups", "rows"), None, None),
        check_vma=False,
    )
```

```python
import functools

import jax
import jax.numpy as jnp
from jax import lax
from jax.experimental import pallas as pl
from jax.experimental.pallas import tpu as pltpu
from jax.sharding import PartitionSpec as P

leakage = 0.01
bf16, f32 = jnp.bfloat16, jnp.float32
VMEM_LIMIT = 56 * 2**20


def iota(shape, axis):
    return lax.broadcasted_iota(jnp.int32, shape, axis)


def one_hot(mask):
    return jnp.where(mask, 1.0, 0.0).astype(bf16)


def dot(a, b):
    return jnp.dot(a, b, preferred_element_type=f32)


def spread(total, channels, offset, copies):
    shape = (total, copies * channels)
    return one_hot((iota(shape, 1) & (channels - 1)) + offset == iota(shape, 0))


def band(target, tap, outs, ins, depth):
    block = iota((outs, depth * ins), 1) // ins
    zero = jnp.zeros((outs, depth * ins), f32)
    for a in range(3):
        for c in range(3):
            taps = [tap(a, b, c) for b in range(3)]
            for z in range(depth):
                rows = zero
                for b in range(3):
                    if 0 <= z + b - 1 < depth:
                        rows = jnp.where(block == z + b - 1, taps[b], rows)
                start = (c * depth + z) * outs
                target[start : start + outs, a * depth * ins : (a + 1) * depth * ins] = rows.astype(bf16)


def band_kernel(target, kernel_ref, outs, total, ins, offset, depth, turned=False):
    picks = spread(total, ins, offset, depth)

    def tap(a, b, c):
        at = (a * 3 + b) * 3 + c
        if turned:
            block = kernel_ref[at * total : (at + 1) * total, :]
            return lax.dot_general(block, picks, (((0,), (0,)), ((), ())), preferred_element_type=f32)
        return dot(kernel_ref[at * outs : (at + 1) * outs, :], picks)

    band(target, tap, outs, ins, depth)


class Band:
    def __init__(self, main, edge, outs, ins):
        self.main, self.edge, self.outs, self.ins = main, edge, outs, ins

    def build(self, kernel_ref, total, offsets):
        outs, ins = self.outs, self.ins
        slices = 128 // outs
        lanes = slices * ins
        picks = [spread(total, ins, offset, slices) for offset in offsets]
        block = iota((outs, lanes), 1) // ins
        zero = jnp.zeros((outs, lanes), f32)
        count = 3 * outs * slices
        for c in range(3):
            ends = [], []
            for at, pick in enumerate(picks):
                for a in range(3):
                    taps = []
                    for b in range(3):
                        row = ((a * 3 + b) * 3 + c) * outs
                        taps.append(dot(kernel_ref[row : row + outs, :], pick))
                    for k in range(slices):
                        rows = zero
                        for b in range(3):
                            if 0 <= k + b - 1 < slices:
                                rows = jnp.where(block == k + b - 1, taps[b], rows)
                        start, left = (c * slices + k) * outs, (at * 3 + a) * lanes
                        self.main[start : start + outs, left : left + lanes] = rows.astype(bf16)
                    ends[0].append(taps[2])
                    ends[1].append(taps[0])
            for which in range(2):
                base = which * count + c * slices * outs
                inner = (1 - which) * (slices - 1)
                for k in range(slices):
                    start = base + k * outs
                    for left in range(0, len(ends[which]), slices):
                        group = ends[which][left : left + slices]
                        rows = zero
                        if k == inner:
                            for at, taps in enumerate(group):
                                rows = jnp.where(block == at, taps, rows)
                        rows = rows[:, : len(group) * ins].astype(bf16)
                        self.edge[start : start + outs, left * ins : (left + len(group)) * ins] = rows


def block_row(band, sources, cells, at, target, to):
    ins, count = band.ins, band.edge.shape[0] // 2
    lanes = cells // 2
    part = band.outs * (128 // band.outs)
    for which in range(2):
        windows = []
        for first, number in ((which * lanes, lanes), (lanes - which * ins, ins)):
            for rows in sources:
                for a in range(3):
                    from_ = pl.multiple_of((at + a) * cells + first, ins)
                    windows.append(rows[pl.ds(from_, number), :])
        left = jnp.concatenate([band.main[...], band.edge[which * count : (which + 1) * count, :]], axis=1)
        sums = dot(left, jnp.concatenate(windows, axis=0))
        place = pl.multiple_of(to * 2 * part + which * part, part)
        target[pl.ds(place, part), :] = finish(sums, part, sums.shape[1])


def block_rows(band, sources, target, cells, first, step, number, shift):
    def one(at):
        block_row(band, sources, cells, at, target, at + shift)

    if number == 2:
        one(first)
        one(first + step)
    else:

        @pl.loop(0, number // 2)
        def _(index):
            one(first + 2 * index * step)
            one(first + (2 * index + 1) * step)


def finish(sums, count, period):
    width = sums.shape[1]
    lane = iota((count, width), 1) & (period - 1)
    left = jnp.where(lane == 0, 0.0, pltpu.roll(sums[:count], 1, 1))
    right = jnp.where(lane == period - 1, 0.0, pltpu.roll(sums[2 * count :], width - 1, 1))
    total = left + sums[count : 2 * count] + right
    return jnp.maximum(total, leakage * total).astype(bf16)


def conv_row(sources, at, count):
    sums = None
    for banded, rows, cells in sources:
        window = rows[pl.ds(pl.multiple_of(at * cells, cells), 3 * cells), :]
        part = dot(banded[...], window)
        sums = part if sums is None else sums + part
    return finish(sums, count, sums.shape[1])


def conv_rows(sources, target, cells, first, step, number, shift):
    def one(at):
        to = pl.multiple_of((at + shift) * cells, cells)
        target[pl.ds(to, cells), :] = conv_row(sources, at, cells)

    if number == 1:
        one(first)
    else:

        @pl.loop(0, number)
        def _(index):
            one(first + index * step)


class Halo:
    def __init__(self, edges, at, buf, cells, source, target, number, step):
        self.edges, self.buf, self.step = edges, buf, step
        self.source = pl.ds(source * cells, number * cells)
        self.target = pl.ds(target * cells, number * cells)
        self.gives, self.takes = edges.has(step), edges.has(-step)
        self.at = at

    def copy(self):
        return pltpu.make_async_remote_copy(
            src_ref=self.buf.at[self.source],
            dst_ref=self.buf.at[self.target],
            send_sem=self.edges.send.at[self.at],
            recv_sem=self.edges.recv.at[self.at],
            device_id=(self.edges.group, self.edges.me + self.step),
            device_id_type=pl.DeviceIdType.MESH,
        )

    def start(self):
        @pl.when(self.gives)
        def _():
            self.copy().start()

    def arrive(self):
        @pl.when(self.takes)
        def _():
            self.copy().wait_recv()

        @pl.when(jnp.logical_not(self.takes))
        def _():
            self.buf[self.target, :] = jnp.zeros((self.target.size, self.buf.shape[1]), bf16)

    def sent(self):
        @pl.when(self.gives)
        def _():
            self.copy().wait_send()


class Edges:
    def __init__(self, groups, rows, count, send, recv):
        self.group, self.me, self.count = lax.axis_index(groups), lax.axis_index(rows), count
        self.send, self.recv = send, recv
        self.halos = []

    def has(self, step):
        other = self.me + step
        return (other >= 0) & (other < self.count)

    def greet(self, others, reach):
        barrier = pltpu.get_barrier_semaphore()

        def signal(to):
            pl.semaphore_signal(barrier, inc=1, device_id=to, device_id_type=pl.DeviceIdType.MESH)

        for other in others:
            signal(other)
        number = len(others)
        for distance in range(1, reach + 1):
            for step in (-distance, distance):

                @pl.when(self.has(step))
                def _():
                    signal((self.group, self.me + step))

                number = number + jnp.where(self.has(step), 1, 0)
        pl.semaphore_wait(barrier, number)

    def pair(self, buf, cells, own, height, number):
        up = Halo(self, len(self.halos), buf, cells, own, own + height, number, -1)
        self.halos.append(up)
        down = Halo(self, len(self.halos), buf, cells, own + height - number, own - number, number, 1)
        self.halos.append(down)
        return [up, down]

    def fan(self, buf, cells, own, reach):
        fans = []
        for distance in range(1, reach + 1):
            for step in (-distance, distance):
                fans.append(Halo(self, len(self.halos), buf, cells, own, own - step, 1, step))
                self.halos.append(fans[-1])
        return fans

    def blank(self, buf, cells, row, step):
        @pl.when(jnp.logical_not(self.has(step)))
        def _():
            buf[row * cells : (row + 1) * cells, :] = jnp.zeros((cells, buf.shape[1]), bf16)


def start(halos):
    for halo in halos:
        halo.start()


def arrive(halos):
    for halo in halos:
        halo.arrive()


class Gather:
    def __init__(self, edges, whole, sems):
        self.edges, self.whole, self.sems = edges, whole, sems
        self.core, self.y, self.z = lax.rem(edges.me, 2), lax.rem(edges.me // 2, 2), edges.me // 4
        self.high = edges.count // 4
        self.cut = whole.shape[1] // 2
        shares = [(y, z) for y in range(2) for z in range(self.high)]
        self.order = sorted(shares, key=lambda s: (bin(s[1]).count("1") + s[0], -s[0], -s[1]))[1:]
        self.started = []
        self.seen = 0

    def device(self, share, other_core=False):
        z = self.z
        for bit in range(self.high.bit_length()):
            if share[1] >> bit & 1:
                size = 2**bit
                z = z + size * (1 - 2 * lax.rem(z // size, 2))
        y = 1 - self.y if share[0] else self.y
        core = 1 - self.core if other_core else self.core
        return (z * 2 + y) * 2 + core

    def bits(self, limit):
        return [2**bit for bit in reversed(range(self.high.bit_length() - 1)) if 2**bit < limit]

    def partners(self):
        group, me = self.edges.group, self.edges.me
        near = [self.device((1, 0))] + [self.device((0, bit)) for bit in self.bits(self.high)]
        return [(1 - group, me)] + [(group, to) for to in near]

    def copy(self, kind, at, slot, half, to):
        group = self.edges.group
        if half is None:
            part = self.whole.at[slot]
        else:
            part = self.whole.at[slot, pl.ds(half * self.cut, self.cut)]
        return pltpu.make_async_remote_copy(
            src_ref=part,
            dst_ref=part,
            send_sem=self.sems[2 * kind].at[at],
            recv_sem=self.sems[2 * kind + 1].at[at],
            device_id=to,
            device_id_type=pl.DeviceIdType.MESH,
        )

    def near(self, share, new, slot_of, to):
        group = self.edges.group
        return self.copy(0, new, self.device(slot_of), group, (group, self.device(to)))

    def swap(self, share, arriving=False):
        group = self.edges.group
        half = 1 - group if arriving else group
        return self.copy(1, share, self.device(share), half, (1 - group, self.edges.me))

    def across(self, which, share, arriving=False):
        group = self.edges.group
        half = None if share == (0, 0) else (1 - group if which else group)
        slot = self.device(share, arriving)
        return self.copy(2, (which,) + share, slot, half, (group, self.device((0, 0), True)))

    def go(self, copy):
        copy.start()
        self.started.append(copy)

    def spread(self, share):
        y, z = share
        if share == (0, 0):
            self.go(self.near(share, (1, 0), share, (1, 0)))
        lowest = z & -z if z else self.high
        for bit in self.bits(lowest):
            self.go(self.near(share, (y, z | bit), share, (0, bit)))
        if share != (0, 0):
            self.go(self.swap(share))
        self.go(self.across(0, share))

    def receive(self, number):
        for share in self.order[self.seen : self.seen + number]:
            self.near(share, share, share, (1, 0)).wait_recv()
            self.spread(share)
        self.seen += number

    def trade(self, first, last):
        for share in self.order[first:last]:
            self.swap(share, True).wait_recv()
            self.go(self.across(1, share))

    def finish(self):
        self.across(0, (0, 0), True).wait_recv()
        for share in self.order:
            for which in range(2):
                self.across(which, share, True).wait_recv()

    def sent(self):
        for copy in self.started:
            copy.wait_send()


def halves(width):
    half = width // 2
    source, target = iota((width, width), 0), iota((width, width), 1)
    return one_hot(source == jnp.where(target < half, 2 * target, 2 * (target - half) + 1))


def weave(width):
    half = width // 2
    source, target = iota((width, width), 0), iota((width, width), 1)
    return one_hot(target == jnp.where(source < half, 2 * source, 2 * (source - half) + 1))


def pool(first, second, chans, parts):
    rows = jnp.maximum(first, second)
    depth, width = rows.shape[0] // chans, rows.shape[1]
    pairs = [
        jnp.maximum(rows[z * chans : (z + 1) * chans], rows[(z + 1) * chans : (z + 2) * chans])
        for z in range(0, depth, 2)
    ]
    split = dot(jnp.concatenate(pairs, axis=0), parts)
    return jnp.maximum(split[:, : width // 2], split[:, width // 2 :]).astype(bf16)


def lift(rows, kernel_ref, ins, outs, woven, store, which=(0, 1)):
    depth = rows.shape[0] // ins
    for a in which:
        kernel = kernel_ref[a * 4 * outs : (a + 1) * 4 * outs, :]
        parts = [dot(kernel, rows[z * ins : (z + 1) * ins]).astype(bf16) for z in range(depth)]
        stack = []
        for z in range(depth):
            for b in range(2):
                at = b * 2 * outs
                stack.append(jnp.concatenate([parts[z][at : at + outs], parts[z][at + outs : at + 2 * outs]], axis=1))
        store(a, dot(jnp.concatenate(stack, axis=0), woven).astype(bf16))


def network(size, groups, rows, count, *refs):
    (vol, b2, b1, k1, k2, k3, k4, ub, mm, mr, um, fm, fr, out) = refs[:14]
    (b_vol, b_one, b_pool, b_first, e1m, e1x, e2m, e2x, e3, e4m, e4x) = refs[14:25]
    (b_fine, b_mid, b_low, b_bot, bot, b_lift, b_three, four, b_raise, b_last) = refs[25:35]
    (kt, t1, t2, t3m, t3x, t4m, t4x, t5m, t5x, t6m, t6x, whole) = refs[35:47]
    (send, recv, *moves, local) = refs[47:]
    H, Z, W, C1, C2, C3 = size
    R, R2, RP, RB = Z * C1, Z // 2 * C2, Z // 4 * C2, Z // 4 * C3
    RQ = Z // 2 * C1
    H2 = H // 2
    side = C3 // C2
    each = -(-27 // side)
    edges = Edges(groups, rows, count, send, recv)
    gather = Gather(edges, whole, moves)
    shares = len(gather.order)
    part = -(-shares // 4)
    vol_halo = edges.pair(b_vol, R, 1, H, 1)
    one_halo = edges.pair(b_one, R, 1, H, 1)
    pool_halo = edges.pair(b_pool, RQ, 2, H2, 2)
    low_halo = edges.fan(b_low, RP, 3, 3)
    mid_halo = edges.pair(b_mid, R2, 2, H2, 2)
    fine_halo = edges.pair(b_fine, R, 2, H, 2)
    four_halo = edges.pair(four, R2, 1, H2, 1)
    e1, e2, e4 = Band(e1m, e1x, C1, C1), Band(e2m, e2x, C1, C1), Band(e4m, e4x, C2, C2)
    t3, t4 = Band(t3m, t3x, C2, C2), Band(t4m, t4x, C2, C2)
    t5, t6 = Band(t5m, t5x, C1, C1), Band(t6m, t6x, C1, C1)
    loads = [
        pltpu.make_async_copy(vol, b_vol.at[pl.ds(R, H * R)], local.at[0]),
        pltpu.make_async_copy(b2, whole.at[edges.me, pl.ds(0, 27)], local.at[1]),
    ]
    for load in loads:
        load.start()
    for t in range(each):
        taps = [b1[q * each + t] if q * each + t < 27 else jnp.zeros(b1.shape[1:], bf16) for q in range(side)]
        whole[edges.me, 27 + t] = jnp.concatenate(taps, axis=-1)
    edges.greet(gather.partners(), 3)
    loads[0].wait()
    start(vol_halo)
    loads[1].wait()
    gather.spread((0, 0))
    e1.build(k1, C1, [0])
    block_rows(e1, [b_vol], b_one, R, 1, 1, H - 2, 1)
    e2.build(k2, C1, [0])
    band_kernel(e3, k3, C2, C1, C1, 0, Z // 2, True)
    arrive(vol_halo)
    block_rows(e1, [b_vol], b_one, R, 0, H - 1, 2, 1)
    start(one_halo)
    gather.receive(part)
    block_rows(e2, [b_one], b_fine, R, 1, 1, H - 2, 2)
    e4.build(k4, C2, [0])
    t3.build(mm, 2 * C2, [0, C2])
    gather.receive(part)
    arrive(one_halo)
    block_rows(e2, [b_one], b_fine, R, 0, H - 1, 2, 2)
    parts = halves(W)
    for h in range(H2):
        first, second = b_fine[(2 * h + 2) * R : (2 * h + 3) * R, :], b_fine[(2 * h + 3) * R : (2 * h + 4) * R, :]
        b_pool[(h + 2) * RQ : (h + 3) * RQ, :] = pool(first, second, C1, parts)
    start(pool_halo)
    gather.receive(part)
    t4.build(mr, C2, [0])
    t5.build(fm, 2 * C1, [0, C1])
    t6.build(fr, C1, [0])
    gather.receive(shares - 3 * part)
    gather.trade(0, shares // 2)
    arrive(pool_halo)
    conv_rows([(e3, b_pool, RQ)], b_first, R2, 0, 1, H2 + 2, 0)
    edges.blank(b_first, R2, 0, -1)
    edges.blank(b_first, R2, H2 + 1, 1)
    block_rows(e4, [b_first], b_mid, R2, 0, 1, H2, 2)
    first, second = b_mid[2 * R2 : 3 * R2, :], b_mid[3 * R2 : 4 * R2, :]
    b_low[3 * RP : 4 * RP, :] = pool(first, second, C2, halves(W // 2))
    start(low_halo)
    start(mid_halo)
    start(fine_halo)
    gather.trade(shares // 2, shares)
    gather.finish()
    wide = Z // 4 * C2
    shape = (C3, side * wide)
    picks = one_hot(iota(shape, 0) == iota(shape, 1) // wide * C2 + (iota(shape, 1) & (C2 - 1)))
    for t in range(each):
        taps = dot(whole[:, 27 + t].reshape(C3, C3), picks).astype(bf16)
        for q in range(side):
            if q * each + t < 27:
                at = (q * each + t) * C3
                kt[at : at + C3, :] = taps[:, q * wide : (q + 1) * wide]

    def tap(a, b, c):
        at = ((a * 3 + b) * 3 + c) * C3
        return kt[at : at + C3, :].astype(f32)

    band(t1, tap, C3, C2, Z // 4)
    for a in range(3):
        for c in range(3):
            for z in range(Z // 4):
                for y in range(Z // 4):
                    r, l = (c * (Z // 4) + z) * C3, (a * (Z // 4) + y) * C3
                    if -1 <= y - z <= 1:
                        t2[r : r + C3, l : l + C3] = whole[:, (a * 3 + y - z + 1) * 3 + c].reshape(C3, C3)
                    else:
                        t2[r : r + C3, l : l + C3] = jnp.zeros((C3, C3), bf16)
    arrive(low_halo)
    narrow = W // 4

    def bottom(banded, source, cells, target, number):
        rows = jnp.concatenate([source[at * cells : (at + 3) * cells, :] for at in range(number)], axis=1)
        for z in range(Z // 4):
            sums = [dot(banded[(c * (Z // 4) + z) * C3 : (c * (Z // 4) + z + 1) * C3, :], rows) for c in range(3)]
            done = finish(jnp.concatenate(sums, axis=0), C3, narrow)
            for at in range(number):
                target[at * RB + z * C3 : at * RB + (z + 1) * C3, :] = done[:, at * narrow : (at + 1) * narrow]

    bottom(t1, b_low, RP, b_bot, 5)
    for step in (-2, -1, 1, 2):
        edges.blank(b_bot, RB, 2 + step, step)
    bottom(t2, b_bot, RB, bot, 3)
    for step in (-1, 1):
        edges.blank(bot, RB, 1 + step, step)
    woven = weave(W // 2)
    for h in range(3):

        def store(a, value):
            at = (2 * h + a) * R2
            b_lift[at : at + R2, :] = value

        lift(bot[h * RB : (h + 1) * RB, :], ub, C3, C2, woven, store)
    arrive(mid_halo)
    block_rows(t3, [b_mid, b_lift], b_three, R2, 0, 1, H2 + 2, 0)
    edges.blank(b_three, R2, 0, -1)
    edges.blank(b_three, R2, H2 + 1, 1)
    block_rows(t4, [b_three], four, R2, 0, 1, H2, 1)
    start(four_halo)
    woven = weave(W)

    def raise_row(h, which=(0, 1)):
        def store(a, value):
            at = (2 * h + a) * R
            b_raise[at : at + R, :] = value

        lift(four[h * R2 : (h + 1) * R2, :], um, C2, C1, woven, store, which)

    for h in range(1, H2 + 1):
        raise_row(h)
    sources = [b_fine, b_raise]
    block_rows(t5, sources, b_last, R, 2, 1, H - 2, 0)
    arrive(four_halo)
    arrive(fine_halo)
    raise_row(0)
    raise_row(H2 + 1)
    block_rows(t5, sources, b_last, R, 0, 1, 2, 0)
    block_rows(t5, sources, b_last, R, H, 1, 2, 0)
    edges.blank(b_last, R, 0, -1)
    edges.blank(b_last, R, H + 1, 1)
    block_rows(t6, [b_last], out, R, 0, 1, H, 0)
    for halo in edges.halos:
        halo.sent()
    gather.sent()


def per_device(count, *args):
    (volume, f1, f2, m1, m2, b1, b2, ub, mm, mr, um, fm, fr) = args
    C1, H, Z, W = volume.shape
    C2, C3 = m1.shape[3], b2.shape[4]
    own = b1.shape[3]
    R, R2, RP, RL, RB = Z * C1, Z // 2 * C2, Z // 2 * C1, Z // 4 * C2, Z // 4 * C3
    H2, W2, W4 = H // 2, W // 2, W // 4
    flat = lambda k: k.reshape(-1, k.shape[-1])
    each = -(-27 // (C3 // C2))
    taps = 27 + each + (27 + each) % 2
    high = count // 4
    cells = volume.transpose(1, 2, 0, 3).reshape(H * R, W)
    vmem, hbm = pl.BlockSpec(memory_space=pltpu.VMEM), pl.BlockSpec(memory_space=pl.ANY)
    V = lambda *shape: pltpu.VMEM(shape, bf16)
    B = lambda ins, number: (V(384, 384 * number), V(768, 3 * ins * number))
    D = pltpu.SemaphoreType.DMA
    assert H == 4 and Z * C1 == 256 and Z // 2 * C2 == 256
    out = pl.pallas_call(
        functools.partial(network, (H, Z, W, C1, C2, C3), "groups", "rows", count),
        out_shape=jax.ShapeDtypeStruct((H * R, W), bf16),
        in_specs=[hbm] * 2 + [vmem] * 11,
        out_specs=vmem,
        scratch_shapes=[
            V((H + 2) * R, W), V((H + 2) * R, W), V((H2 + 4) * RP, W2), V((H2 + 2) * R2, W2),
            *B(C1, 1), *B(C1, 1), V(3 * R2, 3 * RP), *B(C2, 1),
            V((H + 4) * R, W), V((H2 + 4) * R2, W2), V(7 * RL, W4), V(5 * RB, W4), V(3 * RB, W4),
            V((H2 + 4) * R2, W2), V((H2 + 2) * R2, W2), V((H2 + 2) * R2, W2), V((H + 4) * R, W), V((H + 2) * R, W),
            V(27 * C3, Z // 4 * C2), V(3 * RB, 3 * RL), V(3 * RB, 3 * RB), *B(C2, 2),
            *B(C2, 1), *B(C1, 2), *B(C1, 1), V(count, taps, own, C3),
            D((18,)), D((18,)), D((2, high)), D((2, high)), D((2, high)), D((2, high)), D((2, 2, high)), D((2, 2, high)), D((2,)),
        ],
        compiler_params=pltpu.CompilerParams(collective_id=0, has_side_effects=True, vmem_limit_bytes=VMEM_LIMIT),
        name="network",
    )(
        cells, b2.reshape(27, own, C3), b1.reshape(27, own, C2), flat(f1), flat(f2), flat(m1.swapaxes(3, 4)), flat(m2),
        flat(ub), flat(mm), flat(mr), flat(um), flat(fm), flat(fr),
    )
    return out.reshape(H, Z, C1, W).transpose(2, 0, 1, 3)


def solution(mesh):
    placed = [P(None, ("groups", "rows"), None, None)] + [P()] * 12
    placed[5] = placed[6] = P(None, None, None, "rows", None)
    return jax.shard_map(
        functools.partial(per_device, mesh.shape["rows"]),
        mesh=mesh,
        in_specs=tuple(placed),
        out_specs=P(None, ("groups", "rows"), None, None),
        check_vma=False,
    )
```

```python
import functools

import jax
import jax.numpy as jnp
from jax import lax
from jax.experimental import pallas as pl
from jax.experimental.pallas import tpu as pltpu
from jax.sharding import PartitionSpec as P

leakage = 0.01
bf16, f32 = jnp.bfloat16, jnp.float32
VMEM_LIMIT = 56 * 2**20


def iota(shape, axis):
    return lax.broadcasted_iota(jnp.int32, shape, axis)


def one_hot(mask):
    return jnp.where(mask, 1.0, 0.0).astype(bf16)


def dot(a, b):
    return jnp.dot(a, b, preferred_element_type=f32)


def spread(total, channels, offset, copies):
    shape = (total, copies * channels)
    return one_hot((iota(shape, 1) & (channels - 1)) + offset == iota(shape, 0))


def band(target, tap, outs, ins, depth):
    block = iota((outs, depth * ins), 1) // ins
    zero = jnp.zeros((outs, depth * ins), f32)
    for a in range(3):
        for c in range(3):
            taps = [tap(a, b, c) for b in range(3)]
            for z in range(depth):
                rows = zero
                for b in range(3):
                    if 0 <= z + b - 1 < depth:
                        rows = jnp.where(block == z + b - 1, taps[b], rows)
                start = (c * depth + z) * outs
                target[start : start + outs, a * depth * ins : (a + 1) * depth * ins] = rows.astype(bf16)


def band_kernel(target, kernel_ref, outs, total, ins, offset, depth, turned=False):
    picks = spread(total, ins, offset, depth)

    def tap(a, b, c):
        at = (a * 3 + b) * 3 + c
        if turned:
            block = kernel_ref[at * total : (at + 1) * total, :]
            return lax.dot_general(block, picks, (((0,), (0,)), ((), ())), preferred_element_type=f32)
        return dot(kernel_ref[at * outs : (at + 1) * outs, :], picks)

    band(target, tap, outs, ins, depth)


class Band:
    def __init__(self, main, edge, outs, ins):
        self.main, self.edge, self.outs, self.ins = main, edge, outs, ins

    def build(self, kernel_ref, total, offsets):
        outs, ins = self.outs, self.ins
        slices = 128 // outs
        lanes = slices * ins
        picks = [spread(total, ins, offset, slices) for offset in offsets]
        block = iota((outs, lanes), 1) // ins
        zero = jnp.zeros((outs, lanes), f32)
        count = 3 * outs * slices
        for c in range(3):
            ends = [], []
            for at, pick in enumerate(picks):
                for a in range(3):
                    taps = []
                    for b in range(3):
                        row = ((a * 3 + b) * 3 + c) * outs
                        taps.append(dot(kernel_ref[row : row + outs, :], pick))
                    for k in range(slices):
                        rows = zero
                        for b in range(3):
                            if 0 <= k + b - 1 < slices:
                                rows = jnp.where(block == k + b - 1, taps[b], rows)
                        start, left = (c * slices + k) * outs, (at * 3 + a) * lanes
                        self.main[start : start + outs, left : left + lanes] = rows.astype(bf16)
                    ends[0].append(taps[2])
                    ends[1].append(taps[0])
            for which in range(2):
                base = which * count + c * slices * outs
                inner = (1 - which) * (slices - 1)
                for k in range(slices):
                    start = base + k * outs
                    for left in range(0, len(ends[which]), slices):
                        group = ends[which][left : left + slices]
                        rows = zero
                        if k == inner:
                            for at, taps in enumerate(group):
                                rows = jnp.where(block == at, taps, rows)
                        rows = rows[:, : len(group) * ins].astype(bf16)
                        self.edge[start : start + outs, left * ins : (left + len(group)) * ins] = rows


def block_row(band, sources, cells, at, target, to):
    ins, count = band.ins, band.edge.shape[0] // 2
    lanes = cells // 2
    part = band.outs * (128 // band.outs)
    for which in range(2):
        windows = []
        for first, number in ((which * lanes, lanes), (lanes - which * ins, ins)):
            for rows in sources:
                for a in range(3):
                    from_ = pl.multiple_of((at + a) * cells + first, ins)
                    windows.append(rows[pl.ds(from_, number), :])
        left = jnp.concatenate([band.main[...], band.edge[which * count : (which + 1) * count, :]], axis=1)
        sums = dot(left, jnp.concatenate(windows, axis=0))
        place = pl.multiple_of(to * 2 * part + which * part, part)
        target[pl.ds(place, part), :] = finish(sums, part, sums.shape[1])


def block_rows(band, sources, target, cells, first, step, number, shift):
    def one(at):
        block_row(band, sources, cells, at, target, at + shift)

    if number == 2:
        one(first)
        one(first + step)
    else:

        @pl.loop(0, number // 2)
        def _(index):
            one(first + 2 * index * step)
            one(first + (2 * index + 1) * step)


def finish(sums, count, period):
    width = sums.shape[1]
    lane = iota((count, width), 1) & (period - 1)
    left = jnp.where(lane == 0, 0.0, pltpu.roll(sums[:count], 1, 1))
    right = jnp.where(lane == period - 1, 0.0, pltpu.roll(sums[2 * count :], width - 1, 1))
    total = left + sums[count : 2 * count] + right
    return jnp.maximum(total, leakage * total).astype(bf16)


def conv_row(sources, at, count):
    sums = None
    for banded, rows, cells in sources:
        window = rows[pl.ds(pl.multiple_of(at * cells, cells), 3 * cells), :]
        part = dot(banded[...], window)
        sums = part if sums is None else sums + part
    return finish(sums, count, sums.shape[1])


def conv_rows(sources, target, cells, first, step, number, shift):
    def one(at):
        to = pl.multiple_of((at + shift) * cells, cells)
        target[pl.ds(to, cells), :] = conv_row(sources, at, cells)

    if number == 1:
        one(first)
    else:

        @pl.loop(0, number)
        def _(index):
            one(first + index * step)


class Halo:
    def __init__(self, edges, at, buf, cells, source, target, number, step, outside=None):
        self.edges, self.buf, self.step = edges, buf, step
        self.target = pl.ds(target * cells, number * cells)
        self.source = buf.at[pl.ds(source * cells, number * cells)] if outside is None else outside
        self.gives, self.takes = edges.has(step), edges.has(-step)
        self.at = at

    def copy(self):
        return pltpu.make_async_remote_copy(
            src_ref=self.source,
            dst_ref=self.buf.at[self.target.start] if len(self.buf.shape) > 2 else self.buf.at[self.target],
            send_sem=self.edges.send.at[self.at],
            recv_sem=self.edges.recv.at[self.at],
            device_id=(self.edges.group, self.edges.me + self.step),
            device_id_type=pl.DeviceIdType.MESH,
        )

    def start(self):
        @pl.when(self.gives)
        def _():
            self.copy().start()

    def arrive(self):
        @pl.when(self.takes)
        def _():
            self.copy().wait_recv()

        @pl.when(jnp.logical_not(self.takes))
        def _():
            self.buf[self.target] = jnp.zeros((self.target.size,) + self.buf.shape[1:], bf16)

    def sent(self):
        @pl.when(self.gives)
        def _():
            self.copy().wait_send()


class Edges:
    def __init__(self, groups, rows, count, send, recv):
        self.group, self.me, self.count = lax.axis_index(groups), lax.axis_index(rows), count
        self.send, self.recv = send, recv
        self.halos = []

    def has(self, step):
        other = self.me + step
        return (other >= 0) & (other < self.count)

    def greet(self, others, reach):
        barrier = pltpu.get_barrier_semaphore()

        def signal(to):
            pl.semaphore_signal(barrier, inc=1, device_id=to, device_id_type=pl.DeviceIdType.MESH)

        for other in others:
            signal(other)
        number = len(others)
        for distance in range(1, reach + 1):
            for step in (-distance, distance):

                @pl.when(self.has(step))
                def _():
                    signal((self.group, self.me + step))

                number = number + jnp.where(self.has(step), 1, 0)
        pl.semaphore_wait(barrier, number)

    def pair(self, buf, cells, own, height, number, outside=(None, None)):
        up = Halo(self, len(self.halos), buf, cells, own, own + height, number, -1, outside[0])
        self.halos.append(up)
        down = Halo(self, len(self.halos), buf, cells, own + height - number, own - number, number, 1, outside[1])
        self.halos.append(down)
        return [up, down]

    def fan(self, buf, cells, own, reach):
        fans = []
        for distance in range(1, reach + 1):
            for step in (-distance, distance):
                fans.append(Halo(self, len(self.halos), buf, cells, own, own - step, 1, step))
                self.halos.append(fans[-1])
        return fans

    def blank(self, buf, cells, row, step):
        @pl.when(jnp.logical_not(self.has(step)))
        def _():
            buf[row * cells : (row + 1) * cells, :] = jnp.zeros((cells, buf.shape[1]), bf16)


def start(halos):
    for halo in halos:
        halo.start()


def arrive(halos):
    for halo in halos:
        halo.arrive()


class Gather:
    def __init__(self, edges, whole, sems):
        self.edges, self.whole, self.sems = edges, whole, sems
        self.core, self.y, self.z = lax.rem(edges.me, 2), lax.rem(edges.me // 2, 2), edges.me // 4
        self.high = edges.count // 4
        self.cut = whole.shape[1] // 2
        shares = [(y, z) for y in range(2) for z in range(self.high)]
        self.order = sorted(shares, key=lambda s: (bin(s[1]).count("1") + s[0], -s[0], -s[1]))[1:]
        self.started = []
        self.seen = 0

    def device(self, share, other_core=False):
        z = self.z
        for bit in range(self.high.bit_length()):
            if share[1] >> bit & 1:
                size = 2**bit
                z = z + size * (1 - 2 * lax.rem(z // size, 2))
        y = 1 - self.y if share[0] else self.y
        core = 1 - self.core if other_core else self.core
        return (z * 2 + y) * 2 + core

    def bits(self, limit):
        return [2**bit for bit in reversed(range(self.high.bit_length() - 1)) if 2**bit < limit]

    def partners(self):
        group, me = self.edges.group, self.edges.me
        near = [self.device((1, 0))] + [self.device((0, bit)) for bit in self.bits(self.high)]
        return [(1 - group, me)] + [(group, to) for to in near]

    def copy(self, kind, at, slot, half, to):
        group = self.edges.group
        if half is None:
            part = self.whole.at[slot]
        else:
            part = self.whole.at[slot, pl.ds(half * self.cut, self.cut)]
        return pltpu.make_async_remote_copy(
            src_ref=part,
            dst_ref=part,
            send_sem=self.sems[2 * kind].at[at],
            recv_sem=self.sems[2 * kind + 1].at[at],
            device_id=to,
            device_id_type=pl.DeviceIdType.MESH,
        )

    def near(self, share, new, slot_of, to):
        group = self.edges.group
        return self.copy(0, new, self.device(slot_of), group, (group, self.device(to)))

    def swap(self, share, arriving=False):
        group = self.edges.group
        half = 1 - group if arriving else group
        return self.copy(1, share, self.device(share), half, (1 - group, self.edges.me))

    def across(self, which, share, arriving=False):
        group = self.edges.group
        half = None if share == (0, 0) else (1 - group if which else group)
        slot = self.device(share, arriving)
        return self.copy(2, (which,) + share, slot, half, (group, self.device((0, 0), True)))

    def go(self, copy):
        copy.start()
        self.started.append(copy)

    def spread(self, share):
        y, z = share
        lowest = z & -z if z else self.high
        for bit in self.bits(lowest):
            self.go(self.near(share, (y, z | bit), share, (0, bit)))
        if share != (0, 0):
            self.go(self.swap(share))
        self.go(self.across(0, share))

    def sideways(self):
        self.go(self.near((0, 0), (1, 0), (0, 0), (1, 0)))

    def receive(self, number):
        for share in self.order[self.seen : self.seen + number]:
            self.near(share, share, share, (1, 0)).wait_recv()
            self.spread(share)
        self.seen += number

    def trade(self, first, last):
        for share in self.order[first:last]:
            self.swap(share, True).wait_recv()
            self.go(self.across(1, share))

    def finish(self):
        self.across(0, (0, 0), True).wait_recv()
        for share in self.order:
            for which in range(2):
                self.across(which, share, True).wait_recv()

    def sent(self):
        for copy in self.started:
            copy.wait_send()


def halves(width):
    half = width // 2
    source, target = iota((width, width), 0), iota((width, width), 1)
    return one_hot(source == jnp.where(target < half, 2 * target, 2 * (target - half) + 1))


def weave(width):
    half = width // 2
    source, target = iota((width, width), 0), iota((width, width), 1)
    return one_hot(target == jnp.where(source < half, 2 * source, 2 * (source - half) + 1))


def pool(first, second, chans, parts):
    rows = jnp.maximum(first, second)
    depth, width = rows.shape[0] // chans, rows.shape[1]
    pairs = [
        jnp.maximum(rows[z * chans : (z + 1) * chans], rows[(z + 1) * chans : (z + 2) * chans])
        for z in range(0, depth, 2)
    ]
    split = dot(jnp.concatenate(pairs, axis=0), parts)
    return jnp.maximum(split[:, : width // 2], split[:, width // 2 :]).astype(bf16)


def lift(rows, kernel_ref, ins, outs, woven, store, which=(0, 1)):
    depth = rows.shape[0] // ins
    for a in which:
        kernel = kernel_ref[a * 4 * outs : (a + 1) * 4 * outs, :]
        parts = [dot(kernel, rows[z * ins : (z + 1) * ins]).astype(bf16) for z in range(depth)]
        stack = []
        for z in range(depth):
            for b in range(2):
                at = b * 2 * outs
                stack.append(jnp.concatenate([parts[z][at : at + outs], parts[z][at + outs : at + 2 * outs]], axis=1))
        store(a, dot(jnp.concatenate(stack, axis=0), woven).astype(bf16))


def network(size, groups, rows, count, *refs):
    vol, b2, out = refs[0], refs[1], refs[13]
    given, held, refs = refs[2:13], refs[14:25], refs[:14] + refs[25:]
    (b1, k1, k2, k3, k4, ub, mm, mr, um, fm, fr) = held
    (b_vol, b_one, b_pool, b_first, e1m, e1x, e2m, e2x, e3, e4m, e4x) = refs[14:25]
    raw, ready = refs[-3:-1]
    (b_fine, b_mid, b_low, b_bot, bot, b_lift, b_three, four, b_raise, b_last) = refs[25:35]
    (kt, t1, t2, t3m, t3x, t4m, t4x, t5m, t5x, t6m, t6x, whole) = refs[35:47]
    (send, recv, *moves, _, _, local) = refs[47:]
    H, Z, W, C1, C2, C3 = size
    R, R2, RP, RB = Z * C1, Z // 2 * C2, Z // 4 * C2, Z // 4 * C3
    RQ = Z // 2 * C1
    H2 = H // 2
    side = C3 // C2
    each = -(-27 // side)
    edges = Edges(groups, rows, count, send, recv)
    gather = Gather(edges, whole, moves)
    shares = len(gather.order)
    part = -(-shares // 4)
    vol_halo = edges.pair(raw, 1, 1, H, 1, (vol.at[:, 0], vol.at[:, H - 1]))
    one_halo = edges.pair(b_one, R, 1, H, 1)
    pool_halo = edges.pair(b_pool, RQ, 2, H2, 2)
    low_halo = edges.fan(b_low, RP, 3, 3)
    mid_halo = edges.pair(b_mid, R2, 2, H2, 2)
    fine_near = [Halo(edges, 16, b_fine, R, 2, H + 2, 1, -1), Halo(edges, 17, b_fine, R, H + 1, 1, 1, 1)]
    fine_far = [Halo(edges, 18, b_fine, R, 3, H + 3, 1, -1), Halo(edges, 19, b_fine, R, H, 0, 1, 1)]
    four_halo = edges.pair(four, R2, 1, H2, 1)
    assert len(edges.halos) == 16
    edges.halos += fine_near + fine_far
    e1, e2, e4 = Band(e1m, e1x, C1, C1), Band(e2m, e2x, C1, C1), Band(e4m, e4x, C2, C2)
    t3, t4 = Band(t3m, t3x, C2, C2), Band(t4m, t4x, C2, C2)
    t5, t6 = Band(t5m, t5x, C1, C1), Band(t6m, t6x, C1, C1)
    loads = [pltpu.make_async_copy(b2, whole.at[edges.me, pl.ds(0, 27)], local.at[0])]
    loads += [pltpu.make_async_copy(vol.at[:, h], raw.at[h + 1], local.at[1 + h]) for h in range(H)]
    weights = [pltpu.make_async_copy(x, y, local.at[1 + H + at]) for at, (x, y) in enumerate(zip(given, held))]
    for load in weights[:1] + loads + weights[1:]:
        load.start()
    weights[0].wait()
    for t in range(each):
        taps = [b1[q * each + t] if q * each + t < 27 else jnp.zeros(b1.shape[1:], bf16) for q in range(side)]
        whole[edges.me, 27 + t] = jnp.concatenate(taps, axis=-1)
    edges.greet(gather.partners(), 3)
    start(vol_halo)
    loads[0].wait()
    gather.sideways()
    gather.spread((0, 0))
    turn = one_hot(iota((R, R), 1) == iota((R, R), 0) % C1 * Z + iota((R, R), 0) // C1)
    turned = one_hot(iota((R, R), 1) == iota((R, R), 0) % Z * C1 + iota((R, R), 0) // Z)

    def settle(row):
        flat = raw[row].astype(f32).reshape(R, W).astype(bf16)
        b_vol[row * R : (row + 1) * R, :] = dot(turn, flat).astype(bf16)

    for h in range(H):
        loads[1 + h].wait()
        settle(h + 1)
    for load in weights[1:]:
        load.wait()
    e1.build(k1, C1, [0])
    block_rows(e1, [b_vol], b_one, R, 1, 1, H - 2, 1)
    e2.build(k2, C1, [0])
    band_kernel(e3, k3, C2, C1, C1, 0, Z // 2, True)
    arrive(vol_halo)
    settle(0)
    settle(H + 1)
    block_row(e1, [b_vol], R, 0, b_one, 1)
    one_halo[0].start()
    block_row(e1, [b_vol], R, H - 1, b_one, H)
    one_halo[1].start()
    gather.receive(part)
    block_rows(e2, [b_one], b_fine, R, 1, 1, H - 2, 2)
    e4.build(k4, C2, [0])
    t3.build(mm, 2 * C2, [0, C2])
    gather.receive(part)
    arrive(one_halo)
    block_rows(e2, [b_one], b_fine, R, 0, H - 1, 2, 2)
    parts = halves(W)
    for h in range(H2):
        first, second = b_fine[(2 * h + 2) * R : (2 * h + 3) * R, :], b_fine[(2 * h + 3) * R : (2 * h + 4) * R, :]
        b_pool[(h + 2) * RQ : (h + 3) * RQ, :] = pool(first, second, C1, parts)
    start(pool_halo)
    gather.receive(part)
    t4.build(mr, C2, [0])
    t5.build(fm, 2 * C1, [0, C1])
    t6.build(fr, C1, [0])
    gather.receive(shares - 3 * part)
    gather.trade(0, shares // 2)
    arrive(pool_halo)
    start(fine_near)
    conv_rows([(e3, b_pool, RQ)], b_first, R2, 0, 1, H2 + 2, 0)
    edges.blank(b_first, R2, 0, -1)
    edges.blank(b_first, R2, H2 + 1, 1)
    block_rows(e4, [b_first], b_mid, R2, 0, 1, H2, 2)
    first, second = b_mid[2 * R2 : 3 * R2, :], b_mid[3 * R2 : 4 * R2, :]
    b_low[3 * RP : 4 * RP, :] = pool(first, second, C2, halves(W // 2))
    start(low_halo)
    start(mid_halo)
    gather.trade(shares // 2, shares)
    gather.finish()
    wide = Z // 4 * C2
    shape = (C3, side * wide)
    picks = one_hot(iota(shape, 0) == iota(shape, 1) // wide * C2 + (iota(shape, 1) & (C2 - 1)))
    for t in range(each):
        taps = dot(whole[:, 27 + t].reshape(C3, C3), picks).astype(bf16)
        for q in range(side):
            if q * each + t < 27:
                at = (q * each + t) * C3
                kt[at : at + C3, :] = taps[:, q * wide : (q + 1) * wide]

    def tap(a, b, c):
        at = ((a * 3 + b) * 3 + c) * C3
        return kt[at : at + C3, :].astype(f32)

    band(t1, tap, C3, C2, Z // 4)
    for a in range(3):
        for c in range(3):
            for z in range(Z // 4):
                for y in range(Z // 4):
                    r, l = (c * (Z // 4) + z) * C3, (a * (Z // 4) + y) * C3
                    if -1 <= y - z <= 1:
                        t2[r : r + C3, l : l + C3] = whole[:, (a * 3 + y - z + 1) * 3 + c].reshape(C3, C3)
                    else:
                        t2[r : r + C3, l : l + C3] = jnp.zeros((C3, C3), bf16)
    arrive(low_halo)
    narrow = W // 4

    def bottom(banded, source, cells, target, number):
        rows = jnp.concatenate([source[at * cells : (at + 3) * cells, :] for at in range(number)], axis=1)
        for z in range(Z // 4):
            sums = [dot(banded[(c * (Z // 4) + z) * C3 : (c * (Z // 4) + z + 1) * C3, :], rows) for c in range(3)]
            done = finish(jnp.concatenate(sums, axis=0), C3, narrow)
            for at in range(number):
                target[at * RB + z * C3 : at * RB + (z + 1) * C3, :] = done[:, at * narrow : (at + 1) * narrow]

    bottom(t1, b_low, RP, b_bot, 5)
    start(fine_far)
    for step in (-2, -1, 1, 2):
        edges.blank(b_bot, RB, 2 + step, step)
    bottom(t2, b_bot, RB, bot, 3)
    for step in (-1, 1):
        edges.blank(bot, RB, 1 + step, step)
    woven = weave(W // 2)
    for h in range(3):

        def store(a, value):
            at = (2 * h + a) * R2
            b_lift[at : at + R2, :] = value

        lift(bot[h * RB : (h + 1) * RB, :], ub, C3, C2, woven, store)
    arrive(mid_halo)
    block_rows(t3, [b_mid, b_lift], b_three, R2, 0, 1, H2 + 2, 0)
    edges.blank(b_three, R2, 0, -1)
    edges.blank(b_three, R2, H2 + 1, 1)
    block_rows(t4, [b_three], four, R2, 0, 1, H2, 1)
    start(four_halo)
    woven = weave(W)

    def raise_row(h, which=(0, 1)):
        def store(a, value):
            at = (2 * h + a) * R
            b_raise[at : at + R, :] = value

        lift(four[h * R2 : (h + 1) * R2, :], um, C2, C1, woven, store, which)

    for h in range(1, H2 + 1):
        raise_row(h)
    sources = [b_fine, b_raise]
    block_rows(t5, sources, b_last, R, 2, 1, H - 2, 0)
    arrive(four_halo)
    arrive(fine_near + fine_far)
    raise_row(0)
    raise_row(H2 + 1)
    block_rows(t5, sources, b_last, R, 0, 1, 2, 0)
    block_rows(t5, sources, b_last, R, H, 1, 2, 0)
    edges.blank(b_last, R, 0, -1)
    edges.blank(b_last, R, H + 1, 1)
    saves = []
    for h in range(H):
        block_row(t6, [b_last], R, h, b_vol, h)
        ready[h] = dot(turned, b_vol[h * R : (h + 1) * R, :]).reshape(C1, Z, W).astype(bf16)
        saves.append(pltpu.make_async_copy(ready.at[h], out.at[:, h], local.at[1 + h]))
        saves[-1].start()
    for save in saves:
        save.wait()
    for halo in edges.halos:
        halo.sent()
    gather.sent()


def per_device(count, *args):
    (volume, f1, f2, m1, m2, b1, b2, ub, mm, mr, um, fm, fr) = args
    C1, H, Z, W = volume.shape
    C2, C3 = m1.shape[3], b2.shape[4]
    own = b1.shape[3]
    R, R2, RP, RL, RB = Z * C1, Z // 2 * C2, Z // 2 * C1, Z // 4 * C2, Z // 4 * C3
    H2, W2, W4 = H // 2, W // 2, W // 4
    flat = lambda k: k.reshape(-1, k.shape[-1])
    each = -(-27 // (C3 // C2))
    taps = 27 + each + (27 + each) % 2
    high = count // 4
    hbm = pl.BlockSpec(memory_space=pl.ANY)
    operands = [
        volume, b2.reshape(27, own, C3), b1.reshape(27, own, C2), flat(f1), flat(f2), flat(m1.swapaxes(3, 4)), flat(m2),
        flat(ub), flat(mm), flat(mr), flat(um), flat(fm), flat(fr),
    ]
    V = lambda *shape: pltpu.VMEM(shape, bf16)
    B = lambda ins, number: (V(384, 384 * number), V(768, 3 * ins * number))
    D = pltpu.SemaphoreType.DMA
    assert H == 4 and Z * C1 == 256 and Z // 2 * C2 == 256
    return pl.pallas_call(
        functools.partial(network, (H, Z, W, C1, C2, C3), "groups", "rows", count),
        out_shape=jax.ShapeDtypeStruct(volume.shape, bf16),
        in_specs=[hbm] * 13,
        out_specs=hbm,
        scratch_shapes=[V(*x.shape) for x in operands[2:]] + [
            V((H + 2) * R, W), V((H + 2) * R, W), V((H2 + 4) * RP, W2), V((H2 + 2) * R2, W2),
            *B(C1, 1), *B(C1, 1), V(3 * R2, 3 * RP), *B(C2, 1),
            V((H + 4) * R, W), V((H2 + 4) * R2, W2), V(7 * RL, W4), V(5 * RB, W4), V(3 * RB, W4),
            V((H2 + 4) * R2, W2), V((H2 + 2) * R2, W2), V((H2 + 2) * R2, W2), V((H + 4) * R, W), V((H + 2) * R, W),
            V(27 * C3, Z // 4 * C2), V(3 * RB, 3 * RL), V(3 * RB, 3 * RB), *B(C2, 2),
            *B(C2, 1), *B(C1, 2), *B(C1, 1), V(count, taps, own, C3),
            D((20,)), D((20,)), D((2, high)), D((2, high)), D((2, high)), D((2, high)), D((2, 2, high)), D((2, 2, high)),
            V(H + 2, C1, Z, W), V(H, C1, Z, W), D((1 + H + 11,)),
        ],
        compiler_params=pltpu.CompilerParams(collective_id=0, has_side_effects=True, vmem_limit_bytes=VMEM_LIMIT),
        name="network",
    )(*operands)


def solution(mesh):
    placed = [P(None, ("groups", "rows"), None, None)] + [P()] * 12
    placed[5] = placed[6] = P(None, None, None, "rows", None)
    return jax.shard_map(
        functools.partial(per_device, mesh.shape["rows"]),
        mesh=mesh,
        in_specs=tuple(placed),
        out_specs=P(None, ("groups", "rows"), None, None),
        check_vma=False,
    )
```

```python
import functools

import jax
import jax.numpy as jnp
from jax import lax
from jax.experimental import pallas as pl
from jax.experimental.pallas import tpu as pltpu
from jax.sharding import PartitionSpec as P

leakage = 0.01
bf16, f32 = jnp.bfloat16, jnp.float32
VMEM_LIMIT = 56 * 2**20


def iota(shape, axis):
    return lax.broadcasted_iota(jnp.int32, shape, axis)


def one_hot(mask):
    return jnp.where(mask, 1.0, 0.0).astype(bf16)


def dot(a, b):
    return jnp.dot(a, b, preferred_element_type=f32)


def spread(total, channels, offset, copies):
    shape = (total, copies * channels)
    return one_hot((iota(shape, 1) & (channels - 1)) + offset == iota(shape, 0))


def band(target, tap, outs, ins, depth):
    block = iota((outs, depth * ins), 1) // ins
    zero = jnp.zeros((outs, depth * ins), f32)
    for a in range(3):
        for c in range(3):
            taps = [tap(a, b, c) for b in range(3)]
            for z in range(depth):
                rows = zero
                for b in range(3):
                    if 0 <= z + b - 1 < depth:
                        rows = jnp.where(block == z + b - 1, taps[b], rows)
                start = (c * depth + z) * outs
                target[start : start + outs, a * depth * ins : (a + 1) * depth * ins] = rows.astype(bf16)


def band_kernel(target, kernel_ref, outs, total, ins, offset, depth, turned=False):
    picks = spread(total, ins, offset, depth)

    def tap(a, b, c):
        at = (a * 3 + b) * 3 + c
        if turned:
            block = kernel_ref[at * total : (at + 1) * total, :]
            return lax.dot_general(block, picks, (((0,), (0,)), ((), ())), preferred_element_type=f32)
        return dot(kernel_ref[at * outs : (at + 1) * outs, :], picks)

    band(target, tap, outs, ins, depth)


class Band:
    def __init__(self, main, edge, outs, ins):
        self.main, self.edge, self.outs, self.ins = main, edge, outs, ins

    def build(self, kernel_ref, total, offsets):
        outs, ins = self.outs, self.ins
        slices = 128 // outs
        lanes = slices * ins
        picks = [spread(total, ins, offset, slices) for offset in offsets]
        block = iota((outs, lanes), 1) // ins
        zero = jnp.zeros((outs, lanes), f32)
        count = 3 * outs * slices
        for c in range(3):
            ends = [], []
            for at, pick in enumerate(picks):
                for a in range(3):
                    taps = []
                    for b in range(3):
                        row = ((a * 3 + b) * 3 + c) * outs
                        taps.append(dot(kernel_ref[row : row + outs, :], pick))
                    for k in range(slices):
                        rows = zero
                        for b in range(3):
                            if 0 <= k + b - 1 < slices:
                                rows = jnp.where(block == k + b - 1, taps[b], rows)
                        start, left = (c * slices + k) * outs, (at * 3 + a) * lanes
                        self.main[start : start + outs, left : left + lanes] = rows.astype(bf16)
                    ends[0].append(taps[2])
                    ends[1].append(taps[0])
            for which in range(2):
                base = which * count + c * slices * outs
                inner = (1 - which) * (slices - 1)
                for k in range(slices):
                    start = base + k * outs
                    for left in range(0, len(ends[which]), slices):
                        group = ends[which][left : left + slices]
                        rows = zero
                        if k == inner:
                            for at, taps in enumerate(group):
                                rows = jnp.where(block == at, taps, rows)
                        rows = rows[:, : len(group) * ins].astype(bf16)
                        self.edge[start : start + outs, left * ins : (left + len(group)) * ins] = rows


def block_row(band, sources, cells, at, target, to):
    ins, count = band.ins, band.edge.shape[0] // 2
    lanes = cells // 2
    part = band.outs * (128 // band.outs)
    for which in range(2):
        windows = []
        for first, number in ((which * lanes, lanes), (lanes - which * ins, ins)):
            for rows in sources:
                for a in range(3):
                    from_ = pl.multiple_of((at + a) * cells + first, ins)
                    windows.append(rows[pl.ds(from_, number), :])
        left = jnp.concatenate([band.main[...], band.edge[which * count : (which + 1) * count, :]], axis=1)
        sums = dot(left, jnp.concatenate(windows, axis=0))
        place = pl.multiple_of(to * 2 * part + which * part, part)
        target[pl.ds(place, part), :] = finish(sums, part, sums.shape[1])


def block_rows(band, sources, target, cells, first, step, number, shift):
    def one(at):
        block_row(band, sources, cells, at, target, at + shift)

    if number == 2:
        one(first)
        one(first + step)
    else:

        @pl.loop(0, number // 2)
        def _(index):
            one(first + 2 * index * step)
            one(first + (2 * index + 1) * step)


def finish(sums, count, period):
    width = sums.shape[1]
    lane = iota((count, width), 1) & (period - 1)
    left = jnp.where(lane == 0, 0.0, pltpu.roll(sums[:count], 1, 1))
    right = jnp.where(lane == period - 1, 0.0, pltpu.roll(sums[2 * count :], width - 1, 1))
    total = left + sums[count : 2 * count] + right
    return jnp.maximum(total, leakage * total).astype(bf16)


def conv_row(sources, at, count):
    sums = None
    for banded, rows, cells in sources:
        window = rows[pl.ds(pl.multiple_of(at * cells, cells), 3 * cells), :]
        part = dot(banded[...], window)
        sums = part if sums is None else sums + part
    return finish(sums, count, sums.shape[1])


def conv_rows(sources, target, cells, first, step, number, shift):
    def one(at):
        to = pl.multiple_of((at + shift) * cells, cells)
        target[pl.ds(to, cells), :] = conv_row(sources, at, cells)

    if number == 2:
        one(first)
        one(first + step)
    else:

        @pl.loop(0, number // 2)
        def _(index):
            one(first + 2 * index * step)
            one(first + (2 * index + 1) * step)


class Halo:
    def __init__(self, edges, at, buf, cells, source, target, number, step, outside=None):
        self.edges, self.buf, self.step = edges, buf, step
        self.target = pl.ds(target * cells, number * cells)
        self.source = buf.at[pl.ds(source * cells, number * cells)] if outside is None else outside
        self.gives, self.takes = edges.has(step), edges.has(-step)
        self.at = at

    def copy(self):
        return pltpu.make_async_remote_copy(
            src_ref=self.source,
            dst_ref=self.buf.at[self.target.start] if len(self.buf.shape) > 2 else self.buf.at[self.target],
            send_sem=self.edges.send.at[self.at],
            recv_sem=self.edges.recv.at[self.at],
            device_id=(self.edges.group, self.edges.me + self.step),
            device_id_type=pl.DeviceIdType.MESH,
        )

    def start(self):
        @pl.when(self.gives)
        def _():
            self.copy().start()

    def arrive(self):
        @pl.when(self.takes)
        def _():
            self.copy().wait_recv()

        @pl.when(jnp.logical_not(self.takes))
        def _():
            self.buf[self.target] = jnp.zeros((self.target.size,) + self.buf.shape[1:], bf16)

    def sent(self):
        @pl.when(self.gives)
        def _():
            self.copy().wait_send()


class Edges:
    def __init__(self, groups, rows, count, send, recv):
        self.group, self.me, self.count = lax.axis_index(groups), lax.axis_index(rows), count
        self.send, self.recv = send, recv
        self.halos = []

    def has(self, step):
        other = self.me + step
        return (other >= 0) & (other < self.count)

    def greet(self, others, reach):
        barrier = pltpu.get_barrier_semaphore()

        def signal(to):
            pl.semaphore_signal(barrier, inc=1, device_id=to, device_id_type=pl.DeviceIdType.MESH)

        for other in others:
            signal(other)
        number = len(others)
        for distance in range(1, reach + 1):
            for step in (-distance, distance):

                @pl.when(self.has(step))
                def _():
                    signal((self.group, self.me + step))

                number = number + jnp.where(self.has(step), 1, 0)
        pl.semaphore_wait(barrier, number)

    def pair(self, buf, cells, own, height, number, outside=(None, None)):
        up = Halo(self, len(self.halos), buf, cells, own, own + height, number, -1, outside[0])
        self.halos.append(up)
        down = Halo(self, len(self.halos), buf, cells, own + height - number, own - number, number, 1, outside[1])
        self.halos.append(down)
        return [up, down]

    def fan(self, buf, cells, own, reach):
        fans = []
        for distance in range(1, reach + 1):
            for step in (-distance, distance):
                fans.append(Halo(self, len(self.halos), buf, cells, own, own - step, 1, step))
                self.halos.append(fans[-1])
        return fans

    def blank(self, buf, cells, row, step):
        @pl.when(jnp.logical_not(self.has(step)))
        def _():
            buf[row * cells : (row + 1) * cells, :] = jnp.zeros((cells, buf.shape[1]), bf16)


def start(halos):
    for halo in halos:
        halo.start()


def arrive(halos):
    for halo in halos:
        halo.arrive()


class Gather:
    def __init__(self, edges, whole, sems):
        self.edges, self.whole, self.sems = edges, whole, sems
        self.core, self.y, self.z = lax.rem(edges.me, 2), lax.rem(edges.me // 2, 2), edges.me // 4
        self.high = edges.count // 4
        self.cut = whole.shape[1] // 2
        shares = [(y, z) for y in range(2) for z in range(self.high)]
        self.order = sorted(shares, key=lambda s: (bin(s[1]).count("1") + s[0], -s[0], -s[1]))[1:]
        self.started = []
        self.seen = 0

    def device(self, share, other_core=False):
        z = self.z
        for bit in range(self.high.bit_length()):
            if share[1] >> bit & 1:
                size = 2**bit
                z = z + size * (1 - 2 * lax.rem(z // size, 2))
        y = 1 - self.y if share[0] else self.y
        core = 1 - self.core if other_core else self.core
        return (z * 2 + y) * 2 + core

    def bits(self, limit):
        return [2**bit for bit in reversed(range(self.high.bit_length() - 1)) if 2**bit < limit]

    def partners(self):
        group, me = self.edges.group, self.edges.me
        near = [self.device((1, 0))] + [self.device((0, bit)) for bit in self.bits(self.high)]
        return [(1 - group, me)] + [(group, to) for to in near]

    def copy(self, kind, at, slot, half, to):
        group = self.edges.group
        if half is None:
            part = self.whole.at[slot]
        else:
            part = self.whole.at[slot, pl.ds(half * self.cut, self.cut)]
        return pltpu.make_async_remote_copy(
            src_ref=part,
            dst_ref=part,
            send_sem=self.sems[2 * kind].at[at],
            recv_sem=self.sems[2 * kind + 1].at[at],
            device_id=to,
            device_id_type=pl.DeviceIdType.MESH,
        )

    def near(self, share, new, slot_of, to):
        group = self.edges.group
        return self.copy(0, new, self.device(slot_of), group, (group, self.device(to)))

    def swap(self, share, arriving=False):
        group = self.edges.group
        half = 1 - group if arriving else group
        return self.copy(1, share, self.device(share), half, (1 - group, self.edges.me))

    def across(self, which, share, arriving=False):
        group = self.edges.group
        half = None if share == (0, 0) else (1 - group if which else group)
        slot = self.device(share, arriving)
        return self.copy(2, (which,) + share, slot, half, (group, self.device((0, 0), True)))

    def go(self, copy):
        copy.start()
        self.started.append(copy)

    def spread(self, share):
        y, z = share
        lowest = z & -z if z else self.high
        for bit in self.bits(lowest):
            self.go(self.near(share, (y, z | bit), share, (0, bit)))
        if share != (0, 0):
            self.go(self.swap(share))
        self.go(self.across(0, share))

    def sideways(self):
        self.go(self.near((0, 0), (1, 0), (0, 0), (1, 0)))

    def receive(self, number):
        for share in self.order[self.seen : self.seen + number]:
            self.near(share, share, share, (1, 0)).wait_recv()
            self.spread(share)
        self.seen += number

    def trade(self, first, last):
        for share in self.order[first:last]:
            self.swap(share, True).wait_recv()
            self.go(self.across(1, share))

    def finish(self):
        self.across(0, (0, 0), True).wait_recv()
        for share in self.order:
            for which in range(2):
                self.across(which, share, True).wait_recv()

    def sent(self):
        for copy in self.started:
            copy.wait_send()


def halves(width):
    half = width // 2
    source, target = iota((width, width), 0), iota((width, width), 1)
    return one_hot(source == jnp.where(target < half, 2 * target, 2 * (target - half) + 1))


def weave(width):
    half = width // 2
    source, target = iota((width, width), 0), iota((width, width), 1)
    return one_hot(target == jnp.where(source < half, 2 * source, 2 * (source - half) + 1))


def pool(first, second, chans, parts):
    rows = jnp.maximum(first, second)
    depth, width = rows.shape[0] // chans, rows.shape[1]
    pairs = [
        jnp.maximum(rows[z * chans : (z + 1) * chans], rows[(z + 1) * chans : (z + 2) * chans])
        for z in range(0, depth, 2)
    ]
    split = dot(jnp.concatenate(pairs, axis=0), parts)
    return jnp.maximum(split[:, : width // 2], split[:, width // 2 :]).astype(bf16)


def lift(rows, kernel_ref, ins, outs, woven, store, which=(0, 1)):
    depth = rows.shape[0] // ins
    for a in which:
        kernel = kernel_ref[a * 4 * outs : (a + 1) * 4 * outs, :]
        parts = [dot(kernel, rows[z * ins : (z + 1) * ins]).astype(bf16) for z in range(depth)]
        stack = []
        for z in range(depth):
            for b in range(2):
                at = b * 2 * outs
                stack.append(jnp.concatenate([parts[z][at : at + outs], parts[z][at + outs : at + 2 * outs]], axis=1))
        store(a, dot(jnp.concatenate(stack, axis=0), woven).astype(bf16))


def network(size, groups, rows, count, *refs):
    vol, b2, out = refs[0], refs[1], refs[13]
    given, held, refs = refs[2:13], refs[14:25], refs[:14] + refs[25:]
    (b1, k1, k2, k3, k4, ub, mm, mr, um, fm, fr) = held
    (b_vol, b_one, b_pool, b_first, e1m, e1x, e2m, e2x, e3, e4m, e4x) = refs[14:25]
    raw = refs[-2]
    (b_fine, b_mid, b_low, b_bot, bot, b_lift, b_three, four, b_raise, b_last) = refs[25:35]
    (kt, t1, t2, t3m, t3x, t4m, t4x, t5m, t5x, t6m, t6x, whole) = refs[35:47]
    (send, recv, *moves, _, local) = refs[47:]
    H, Z, W, C1, C2, C3 = size
    R, R2, RP, RB = Z * C1, Z // 2 * C2, Z // 4 * C2, Z // 4 * C3
    RQ = Z // 2 * C1
    H2 = H // 2
    side = C3 // C2
    each = -(-27 // side)
    edges = Edges(groups, rows, count, send, recv)
    gather = Gather(edges, whole, moves)
    shares = len(gather.order)
    part = -(-shares // 4)
    vol_halo = edges.pair(raw, 1, 1, H, 1, (vol.at[:, 0], vol.at[:, H - 1]))
    one_halo = edges.pair(b_one, R, 1, H, 1)
    pool_halo = [Halo(edges, 4 + at, b_pool, RQ, 2 + at // 2, 2 + at // 2 + (2 if at % 2 == 0 else -2), 1, -1 if at % 2 == 0 else 1) for at in range(4)]
    edges.halos += pool_halo
    low_halo = edges.fan(b_low, RP, 3, 3)
    mid_halo = edges.pair(b_mid, R2, 2, H2, 2)
    fine_near = [Halo(edges, 18, b_fine, R, 2, H + 2, 1, -1), Halo(edges, 19, b_fine, R, H + 1, 1, 1, 1)]
    fine_far = [Halo(edges, 20, b_fine, R, 3, H + 3, 1, -1), Halo(edges, 21, b_fine, R, H, 0, 1, 1)]
    four_halo = edges.pair(four, R2, 1, H2, 1)
    assert len(edges.halos) == 18
    edges.halos += fine_near + fine_far
    e1, e2, e4 = Band(e1m, e1x, C1, C1), Band(e2m, e2x, C1, C1), Band(e4m, e4x, C2, C2)
    t3, t4 = Band(t3m, t3x, C2, C2), Band(t4m, t4x, C2, C2)
    t5, t6 = Band(t5m, t5x, C1, C1), Band(t6m, t6x, C1, C1)
    loads = [pltpu.make_async_copy(b2, whole.at[edges.me, pl.ds(0, 27)], local.at[0])]
    loads += [pltpu.make_async_copy(vol.at[:, h], raw.at[h + 1], local.at[1 + h]) for h in range(H)]
    weights = [pltpu.make_async_copy(x, y, local.at[1 + H + at]) for at, (x, y) in enumerate(zip(given, held))]
    for load in weights[:1] + loads + weights[1:]:
        load.start()
    weights[0].wait()
    for t in range(each):
        taps = [b1[q * each + t] if q * each + t < 27 else jnp.zeros(b1.shape[1:], bf16) for q in range(side)]
        whole[edges.me, 27 + t] = jnp.concatenate(taps, axis=-1)
    edges.greet(gather.partners(), 3)
    start(vol_halo)
    loads[0].wait()
    gather.sideways()
    gather.spread((0, 0))
    turn = one_hot(iota((R, R), 1) == iota((R, R), 0) % C1 * Z + iota((R, R), 0) // C1)

    def settle(row):
        flat = raw[row].astype(f32).reshape(R, W).astype(bf16)
        b_vol[row * R : (row + 1) * R, :] = dot(turn, flat).astype(bf16)

    for h in range(H):
        loads[1 + h].wait()
        settle(h + 1)
    for load in weights[1:]:
        load.wait()
    e1.build(k1, C1, [0])
    block_rows(e1, [b_vol], b_one, R, 1, 1, H - 2, 1)
    e2.build(k2, C1, [0])
    band_kernel(e3, k3, C2, C1, C1, 0, Z // 2, True)
    arrive(vol_halo)
    settle(0)
    settle(H + 1)
    block_row(e1, [b_vol], R, 0, b_one, 1)
    one_halo[0].start()
    block_row(e1, [b_vol], R, H - 1, b_one, H)
    one_halo[1].start()
    gather.receive(part)
    block_rows(e2, [b_one], b_fine, R, 1, 1, H - 2, 2)
    e4.build(k4, C2, [0])
    t3.build(mm, 2 * C2, [0, C2])
    gather.receive(part)
    arrive(one_halo)
    parts = halves(W)
    for h in range(H2):
        block_row(e2, [b_one], R, h * (H - 1), b_fine, h * (H - 1) + 2)
        first, second = b_fine[(2 * h + 2) * R : (2 * h + 3) * R, :], b_fine[(2 * h + 3) * R : (2 * h + 4) * R, :]
        b_pool[(h + 2) * RQ : (h + 3) * RQ, :] = pool(first, second, C1, parts)
        start(pool_halo[2 * h : 2 * h + 2])
    gather.receive(part)
    t4.build(mr, C2, [0])
    t5.build(fm, 2 * C1, [0, C1])
    t6.build(fr, C1, [0])
    gather.receive(shares - 3 * part)
    arrive(pool_halo)
    start(fine_near)
    conv_rows([(e3, b_pool, RQ)], b_first, R2, 0, 1, H2 + 2, 0)
    gather.trade(0, shares // 2)
    edges.blank(b_first, R2, 0, -1)
    edges.blank(b_first, R2, H2 + 1, 1)
    block_rows(e4, [b_first], b_mid, R2, 0, 1, H2, 2)
    first, second = b_mid[2 * R2 : 3 * R2, :], b_mid[3 * R2 : 4 * R2, :]
    b_low[3 * RP : 4 * RP, :] = pool(first, second, C2, halves(W // 2))
    start(low_halo)
    start(mid_halo)
    gather.trade(shares // 2, shares)
    gather.finish()
    wide = Z // 4 * C2
    shape = (C3, side * wide)
    picks = one_hot(iota(shape, 0) == iota(shape, 1) // wide * C2 + (iota(shape, 1) & (C2 - 1)))
    for t in range(each):
        taps = dot(whole[:, 27 + t].reshape(C3, C3), picks).astype(bf16)
        for q in range(side):
            if q * each + t < 27:
                at = (q * each + t) * C3
                kt[at : at + C3, :] = taps[:, q * wide : (q + 1) * wide]

    def tap(a, b, c):
        at = ((a * 3 + b) * 3 + c) * C3
        return kt[at : at + C3, :].astype(f32)

    band(t1, tap, C3, C2, Z // 4)
    for a in range(3):
        for c in range(3):
            for z in range(Z // 4):
                for y in range(Z // 4):
                    r, l = (c * (Z // 4) + z) * C3, (a * (Z // 4) + y) * C3
                    if -1 <= y - z <= 1:
                        t2[r : r + C3, l : l + C3] = whole[:, (a * 3 + y - z + 1) * 3 + c].reshape(C3, C3)
                    else:
                        t2[r : r + C3, l : l + C3] = jnp.zeros((C3, C3), bf16)
    arrive(low_halo)
    narrow = W // 4

    def bottom(banded, source, cells, target, number):
        rows = jnp.concatenate([source[at * cells : (at + 3) * cells, :] for at in range(number)], axis=1)
        for z in range(Z // 4):
            sums = [dot(banded[(c * (Z // 4) + z) * C3 : (c * (Z // 4) + z + 1) * C3, :], rows) for c in range(3)]
            done = finish(jnp.concatenate(sums, axis=0), C3, narrow)
            for at in range(number):
                target[at * RB + z * C3 : at * RB + (z + 1) * C3, :] = done[:, at * narrow : (at + 1) * narrow]

    bottom(t1, b_low, RP, b_bot, 5)
    start(fine_far)
    for step in (-2, -1, 1, 2):
        edges.blank(b_bot, RB, 2 + step, step)
    bottom(t2, b_bot, RB, bot, 3)
    for step in (-1, 1):
        edges.blank(bot, RB, 1 + step, step)
    woven = weave(W // 2)
    for h in range(3):

        def store(a, value):
            at = (2 * h + a) * R2
            b_lift[at : at + R2, :] = value

        lift(bot[h * RB : (h + 1) * RB, :], ub, C3, C2, woven, store)
    arrive(mid_halo)
    block_rows(t3, [b_mid, b_lift], b_three, R2, 0, 1, H2 + 2, 0)
    edges.blank(b_three, R2, 0, -1)
    edges.blank(b_three, R2, H2 + 1, 1)
    for h in range(H2):
        block_row(t4, [b_three], R2, h, four, h + 1)
        if h == 0:
            four_halo[0].start()
    four_halo[1].start()
    woven = weave(W)

    def raise_row(h, which=(0, 1)):
        def store(a, value):
            at = (2 * h + a) * R
            b_raise[at : at + R, :] = value

        lift(four[h * R2 : (h + 1) * R2, :], um, C2, C1, woven, store, which)

    for h in range(1, H2 + 1):
        raise_row(h)
    sources = [b_fine, b_raise]
    block_rows(t5, sources, b_last, R, 2, 1, H - 2, 0)
    arrive(four_halo)
    arrive(fine_near + fine_far)
    raise_row(0)
    raise_row(H2 + 1)
    block_rows(t5, sources, b_last, R, 0, 1, 2, 0)
    block_rows(t5, sources, b_last, R, H, 1, 2, 0)
    edges.blank(b_last, R, 0, -1)
    edges.blank(b_last, R, H + 1, 1)
    saves = []
    for h in range(H):
        block_row(t6, [b_last], R, h, b_vol, h)
        saves.append(pltpu.make_async_copy(b_vol.at[pl.ds(h * R, R)], out.at[pl.ds(h * R, R)], local.at[1 + h]))
        saves[-1].start()
    for save in saves:
        save.wait()
    for halo in edges.halos:
        halo.sent()
    gather.sent()


def per_device(count, *args):
    (volume, f1, f2, m1, m2, b1, b2, ub, mm, mr, um, fm, fr) = args
    C1, H, Z, W = volume.shape
    C2, C3 = m1.shape[3], b2.shape[4]
    own = b1.shape[3]
    R, R2, RP, RL, RB = Z * C1, Z // 2 * C2, Z // 2 * C1, Z // 4 * C2, Z // 4 * C3
    H2, W2, W4 = H // 2, W // 2, W // 4
    flat = lambda k: k.reshape(-1, k.shape[-1])
    each = -(-27 // (C3 // C2))
    taps = 27 + each + (27 + each) % 2
    high = count // 4
    hbm = pl.BlockSpec(memory_space=pl.ANY)
    operands = [
        volume, b2.reshape(27, own, C3), b1.reshape(27, own, C2), flat(f1), flat(f2), flat(m1.swapaxes(3, 4)), flat(m2),
        flat(ub), flat(mm), flat(mr), flat(um), flat(fm), flat(fr),
    ]
    V = lambda *shape: pltpu.VMEM(shape, bf16)
    B = lambda ins, number: (V(384, 384 * number), V(768, 3 * ins * number))
    D = pltpu.SemaphoreType.DMA
    assert H == 4 and Z * C1 == 256 and Z // 2 * C2 == 256
    out = pl.pallas_call(
        functools.partial(network, (H, Z, W, C1, C2, C3), "groups", "rows", count),
        out_shape=jax.ShapeDtypeStruct((H * R, W), bf16),
        in_specs=[hbm] * 13,
        out_specs=hbm,
        scratch_shapes=[V(*x.shape) for x in operands[2:]] + [
            V((H + 2) * R, W), V((H + 2) * R, W), V((H2 + 4) * RP, W2), V((H2 + 2) * R2, W2),
            *B(C1, 1), *B(C1, 1), V(3 * R2, 3 * RP), *B(C2, 1),
            V((H + 4) * R, W), V((H2 + 4) * R2, W2), V(7 * RL, W4), V(5 * RB, W4), V(3 * RB, W4),
            V((H2 + 4) * R2, W2), V((H2 + 2) * R2, W2), V((H2 + 2) * R2, W2), V((H + 4) * R, W), V((H + 2) * R, W),
            V(27 * C3, Z // 4 * C2), V(3 * RB, 3 * RL), V(3 * RB, 3 * RB), *B(C2, 2),
            *B(C2, 1), *B(C1, 2), *B(C1, 1), V(count, taps, own, C3),
            D((22,)), D((22,)), D((2, high)), D((2, high)), D((2, high)), D((2, high)), D((2, 2, high)), D((2, 2, high)),
            V(H + 2, C1, Z, W), D((1 + H + 11,)),
        ],
        compiler_params=pltpu.CompilerParams(collective_id=0, has_side_effects=True, vmem_limit_bytes=VMEM_LIMIT),
        name="network",
    )(*operands)
    return out.reshape(H, Z, C1, W).transpose(2, 0, 1, 3)


def solution(mesh):
    placed = [P(None, ("groups", "rows"), None, None)] + [P()] * 12
    placed[5] = placed[6] = P(None, None, None, "rows", None)
    return jax.shard_map(
        functools.partial(per_device, mesh.shape["rows"]),
        mesh=mesh,
        in_specs=tuple(placed),
        out_specs=P(None, ("groups", "rows"), None, None),
        check_vma=False,
    )
```

```python
import functools

import jax
import jax.numpy as jnp
from jax import lax
from jax.experimental import pallas as pl
from jax.experimental.pallas import tpu as pltpu
from jax.sharding import PartitionSpec as P

leakage = 0.01
bf16, f32 = jnp.bfloat16, jnp.float32
VMEM_LIMIT = 56 * 2**20


def iota(shape, axis):
    return lax.broadcasted_iota(jnp.int32, shape, axis)


def one_hot(mask):
    return jnp.where(mask, 1.0, 0.0).astype(bf16)


def dot(a, b):
    return jnp.dot(a, b, preferred_element_type=f32)


def spread(total, channels, offset, copies):
    shape = (total, copies * channels)
    return one_hot((iota(shape, 1) & (channels - 1)) + offset == iota(shape, 0))


def band(target, tap, outs, ins, depth):
    block = iota((outs, depth * ins), 1) // ins
    zero = jnp.zeros((outs, depth * ins), f32)
    for a in range(3):
        for c in range(3):
            taps = [tap(a, b, c) for b in range(3)]
            for z in range(depth):
                rows = zero
                for b in range(3):
                    if 0 <= z + b - 1 < depth:
                        rows = jnp.where(block == z + b - 1, taps[b], rows)
                start = (c * depth + z) * outs
                target[start : start + outs, a * depth * ins : (a + 1) * depth * ins] = rows.astype(bf16)


def band_kernel(target, kernel_ref, outs, total, ins, offset, depth, turned=False):
    picks = spread(total, ins, offset, depth)

    def tap(a, b, c):
        at = (a * 3 + b) * 3 + c
        if turned:
            block = kernel_ref[at * total : (at + 1) * total, :]
            return lax.dot_general(block, picks, (((0,), (0,)), ((), ())), preferred_element_type=f32)
        return dot(kernel_ref[at * outs : (at + 1) * outs, :], picks)

    band(target, tap, outs, ins, depth)


class Band:
    def __init__(self, main, edge, outs, ins):
        self.main, self.edge, self.outs, self.ins = main, edge, outs, ins

    def build(self, kernel_ref, total, offsets):
        outs, ins = self.outs, self.ins
        slices = 128 // outs
        lanes = slices * ins
        picks = [spread(total, ins, offset, slices) for offset in offsets]
        block = iota((outs, lanes), 1) // ins
        zero = jnp.zeros((outs, lanes), f32)
        count = 3 * outs * slices
        for c in range(3):
            ends = [], []
            for at, pick in enumerate(picks):
                for a in range(3):
                    taps = []
                    for b in range(3):
                        row = ((a * 3 + b) * 3 + c) * outs
                        taps.append(dot(kernel_ref[row : row + outs, :], pick))
                    for k in range(slices):
                        rows = zero
                        for b in range(3):
                            if 0 <= k + b - 1 < slices:
                                rows = jnp.where(block == k + b - 1, taps[b], rows)
                        start, left = (c * slices + k) * outs, (at * 3 + a) * lanes
                        self.main[start : start + outs, left : left + lanes] = rows.astype(bf16)
                    ends[0].append(taps[2])
                    ends[1].append(taps[0])
            for which in range(2):
                base = which * count + c * slices * outs
                inner = (1 - which) * (slices - 1)
                for k in range(slices):
                    start = base + k * outs
                    for left in range(0, len(ends[which]), slices):
                        group = ends[which][left : left + slices]
                        rows = zero
                        if k == inner:
                            for at, taps in enumerate(group):
                                rows = jnp.where(block == at, taps, rows)
                        rows = rows[:, : len(group) * ins].astype(bf16)
                        self.edge[start : start + outs, left * ins : (left + len(group)) * ins] = rows


def block_row(band, sources, cells, at, target, to):
    ins, count = band.ins, band.edge.shape[0] // 2
    lanes = cells // 2
    part = band.outs * (128 // band.outs)
    for which in range(2):
        windows = []
        for first, number in ((which * lanes, lanes), (lanes - which * ins, ins)):
            for rows in sources:
                for a in range(3):
                    from_ = pl.multiple_of((at + a) * cells + first, ins)
                    windows.append(rows[pl.ds(from_, number), :])
        left = jnp.concatenate([band.main[...], band.edge[which * count : (which + 1) * count, :]], axis=1)
        sums = dot(left, jnp.concatenate(windows, axis=0))
        place = pl.multiple_of(to * 2 * part + which * part, part)
        target[pl.ds(place, part), :] = finish(sums, part, sums.shape[1])


def block_rows(band, sources, target, cells, first, step, number, shift):
    for index in range(number):
        at = first + index * step
        block_row(band, sources, cells, at, target, at + shift)


def finish(sums, count, period):
    width = sums.shape[1]
    lane = iota((count, width), 1) & (period - 1)
    left = jnp.where(lane == 0, 0.0, pltpu.roll(sums[:count], 1, 1))
    right = jnp.where(lane == period - 1, 0.0, pltpu.roll(sums[2 * count :], width - 1, 1))
    total = left + sums[count : 2 * count] + right
    return jnp.maximum(total, leakage * total).astype(bf16)


def conv_row(sources, at, count):
    sums = None
    for banded, rows, cells in sources:
        window = rows[pl.ds(pl.multiple_of(at * cells, cells), 3 * cells), :]
        part = dot(banded[...], window)
        sums = part if sums is None else sums + part
    return finish(sums, count, sums.shape[1])


def conv_rows(sources, target, cells, first, step, number, shift):
    def one(at):
        to = pl.multiple_of((at + shift) * cells, cells)
        target[pl.ds(to, cells), :] = conv_row(sources, at, cells)

    if number == 2:
        one(first)
        one(first + step)
    else:

        @pl.loop(0, number // 2)
        def _(index):
            one(first + 2 * index * step)
            one(first + (2 * index + 1) * step)


class Halo:
    def __init__(self, edges, at, buf, cells, source, target, number, step, outside=None):
        self.edges, self.buf, self.step = edges, buf, step
        self.target = pl.ds(target * cells, number * cells)
        self.source = buf.at[pl.ds(source * cells, number * cells)] if outside is None else outside
        self.gives, self.takes = edges.has(step), edges.has(-step)
        self.at = at

    def copy(self):
        return pltpu.make_async_remote_copy(
            src_ref=self.source,
            dst_ref=self.buf.at[self.target.start] if len(self.buf.shape) > 2 else self.buf.at[self.target],
            send_sem=self.edges.send.at[self.at],
            recv_sem=self.edges.recv.at[self.at],
            device_id=(self.edges.group, self.edges.me + self.step),
            device_id_type=pl.DeviceIdType.MESH,
        )

    def start(self):
        @pl.when(self.gives)
        def _():
            self.copy().start()

    def arrive(self):
        @pl.when(self.takes)
        def _():
            self.copy().wait_recv()

        @pl.when(jnp.logical_not(self.takes))
        def _():
            self.buf[self.target] = jnp.zeros((self.target.size,) + self.buf.shape[1:], bf16)

    def sent(self):
        @pl.when(self.gives)
        def _():
            self.copy().wait_send()


class Edges:
    def __init__(self, groups, rows, count, send, recv):
        self.group, self.me, self.count = lax.axis_index(groups), lax.axis_index(rows), count
        self.send, self.recv = send, recv
        self.halos = []

    def has(self, step):
        other = self.me + step
        return (other >= 0) & (other < self.count)

    def greet(self, others, reach):
        barrier = pltpu.get_barrier_semaphore()

        def signal(to):
            pl.semaphore_signal(barrier, inc=1, device_id=to, device_id_type=pl.DeviceIdType.MESH)

        for other in others:
            signal(other)
        number = len(others)
        for distance in range(1, reach + 1):
            for step in (-distance, distance):

                @pl.when(self.has(step))
                def _():
                    signal((self.group, self.me + step))

                number = number + jnp.where(self.has(step), 1, 0)
        pl.semaphore_wait(barrier, number)

    def pair(self, buf, cells, own, height, number, outside=(None, None)):
        up = Halo(self, len(self.halos), buf, cells, own, own + height, number, -1, outside[0])
        self.halos.append(up)
        down = Halo(self, len(self.halos), buf, cells, own + height - number, own - number, number, 1, outside[1])
        self.halos.append(down)
        return [up, down]

    def fan(self, buf, cells, own, reach):
        fans = []
        for distance in range(1, reach + 1):
            for step in (-distance, distance):
                fans.append(Halo(self, len(self.halos), buf, cells, own, own - step, 1, step))
                self.halos.append(fans[-1])
        return fans

    def blank(self, buf, cells, row, step):
        @pl.when(jnp.logical_not(self.has(step)))
        def _():
            buf[row * cells : (row + 1) * cells, :] = jnp.zeros((cells, buf.shape[1]), bf16)


def start(halos):
    for halo in halos:
        halo.start()


def arrive(halos):
    for halo in halos:
        halo.arrive()


class Gather:
    def __init__(self, edges, whole, sems):
        self.edges, self.whole, self.sems = edges, whole, sems
        self.core, self.y, self.z = lax.rem(edges.me, 2), lax.rem(edges.me // 2, 2), edges.me // 4
        self.high = edges.count // 4
        self.cut = whole.shape[1] // 2
        shares = [(y, z) for y in range(2) for z in range(self.high)]
        self.order = sorted(shares, key=lambda s: (bin(s[1]).count("1") + s[0], -s[0], -s[1]))[1:]
        self.started = []
        self.seen = 0

    def device(self, share, other_core=False):
        z = self.z
        for bit in range(self.high.bit_length()):
            if share[1] >> bit & 1:
                size = 2**bit
                z = z + size * (1 - 2 * lax.rem(z // size, 2))
        y = 1 - self.y if share[0] else self.y
        core = 1 - self.core if other_core else self.core
        return (z * 2 + y) * 2 + core

    def bits(self, limit):
        return [2**bit for bit in reversed(range(self.high.bit_length() - 1)) if 2**bit < limit]

    def partners(self):
        group, me = self.edges.group, self.edges.me
        near = [self.device((1, 0))] + [self.device((0, bit)) for bit in self.bits(self.high)]
        return [(1 - group, me)] + [(group, to) for to in near]

    def copy(self, kind, at, slot, half, to):
        group = self.edges.group
        if half is None:
            part = self.whole.at[slot]
        else:
            part = self.whole.at[slot, pl.ds(half * self.cut, self.cut)]
        return pltpu.make_async_remote_copy(
            src_ref=part,
            dst_ref=part,
            send_sem=self.sems[2 * kind].at[at],
            recv_sem=self.sems[2 * kind + 1].at[at],
            device_id=to,
            device_id_type=pl.DeviceIdType.MESH,
        )

    def near(self, share, new, slot_of, to):
        group = self.edges.group
        return self.copy(0, new, self.device(slot_of), group, (group, self.device(to)))

    def swap(self, share, arriving=False):
        group = self.edges.group
        half = 1 - group if arriving else group
        return self.copy(1, share, self.device(share), half, (1 - group, self.edges.me))

    def across(self, which, share, arriving=False):
        group = self.edges.group
        half = None if share == (0, 0) else (1 - group if which else group)
        slot = self.device(share, arriving)
        return self.copy(2, (which,) + share, slot, half, (group, self.device((0, 0), True)))

    def go(self, copy):
        copy.start()
        self.started.append(copy)

    def spread(self, share):
        y, z = share
        lowest = z & -z if z else self.high
        for bit in self.bits(lowest):
            self.go(self.near(share, (y, z | bit), share, (0, bit)))
        if share != (0, 0):
            self.go(self.swap(share))
        self.go(self.across(0, share))

    def sideways(self):
        self.go(self.near((0, 0), (1, 0), (0, 0), (1, 0)))

    def receive(self, number):
        for share in self.order[self.seen : self.seen + number]:
            self.near(share, share, share, (1, 0)).wait_recv()
            self.spread(share)
        self.seen += number

    def trade(self, first, last):
        for share in self.order[first:last]:
            self.swap(share, True).wait_recv()
            self.go(self.across(1, share))

    def finish(self):
        self.across(0, (0, 0), True).wait_recv()
        for share in self.order:
            for which in range(2):
                self.across(which, share, True).wait_recv()

    def sent(self):
        for copy in self.started:
            copy.wait_send()


def halves(width):
    half = width // 2
    source, target = iota((width, width), 0), iota((width, width), 1)
    return one_hot(source == jnp.where(target < half, 2 * target, 2 * (target - half) + 1))


def weave(width):
    half = width // 2
    source, target = iota((width, width), 0), iota((width, width), 1)
    return one_hot(target == jnp.where(source < half, 2 * source, 2 * (source - half) + 1))


def pool(first, second, chans, parts):
    rows = jnp.maximum(first, second)
    depth, width = rows.shape[0] // chans, rows.shape[1]
    pairs = [
        jnp.maximum(rows[z * chans : (z + 1) * chans], rows[(z + 1) * chans : (z + 2) * chans])
        for z in range(0, depth, 2)
    ]
    split = dot(jnp.concatenate(pairs, axis=0), parts)
    return jnp.maximum(split[:, : width // 2], split[:, width // 2 :]).astype(bf16)


def lift(rows, kernel_ref, ins, outs, woven, store, which=(0, 1)):
    depth = rows.shape[0] // ins
    for a in which:
        kernel = kernel_ref[a * 4 * outs : (a + 1) * 4 * outs, :]
        parts = [dot(kernel, rows[z * ins : (z + 1) * ins]).astype(bf16) for z in range(depth)]
        stack = []
        for z in range(depth):
            for b in range(2):
                at = b * 2 * outs
                stack.append(jnp.concatenate([parts[z][at : at + outs], parts[z][at + outs : at + 2 * outs]], axis=1))
        store(a, dot(jnp.concatenate(stack, axis=0), woven).astype(bf16))


def network(size, groups, rows, count, *refs):
    vol, b2, out = refs[0], refs[1], refs[13]
    given, held, refs = refs[2:13], refs[14:25], refs[:14] + refs[25:]
    (b1, k1, k2, k3, k4, ub, mm, mr, um, fm, fr) = held
    (b_vol, b_one, b_pool, b_first, e1m, e1x, e2m, e2x, e3, e4m, e4x) = refs[14:25]
    raw = refs[-2]
    (b_fine, b_mid, b_low, b_bot, bot, b_lift, b_three, four, b_raise, b_last) = refs[25:35]
    (kt, t1, t2, t3m, t3x, t4m, t4x, t5m, t5x, t6m, t6x, whole) = refs[35:47]
    (send, recv, *moves, _, local) = refs[47:]
    H, Z, W, C1, C2, C3 = size
    R, R2, RP, RB = Z * C1, Z // 2 * C2, Z // 4 * C2, Z // 4 * C3
    RQ = Z // 2 * C1
    H2 = H // 2
    side = C3 // C2
    each = -(-27 // side)
    edges = Edges(groups, rows, count, send, recv)
    gather = Gather(edges, whole, moves)
    shares = len(gather.order)
    part = -(-shares // 4)
    vol_halo = edges.pair(raw, 1, 1, H, 1, (vol.at[:, 0], vol.at[:, H - 1]))
    one_halo = edges.pair(b_one, R, 1, H, 1)
    pool_halo = [Halo(edges, 4 + at, b_pool, RQ, 2 + at // 2, 2 + at // 2 + (2 if at % 2 == 0 else -2), 1, -1 if at % 2 == 0 else 1) for at in range(4)]
    edges.halos += pool_halo
    low_halo = edges.fan(b_low, RP, 3, 3)
    mid_halo = edges.pair(b_mid, R2, 2, H2, 2)
    fine_near = [Halo(edges, 18, b_fine, R, 2, H + 2, 1, -1), Halo(edges, 19, b_fine, R, H + 1, 1, 1, 1)]
    fine_far = [Halo(edges, 20, b_fine, R, 3, H + 3, 1, -1), Halo(edges, 21, b_fine, R, H, 0, 1, 1)]
    four_halo = edges.pair(four, R2, 1, H2, 1)
    assert len(edges.halos) == 18
    edges.halos += fine_near + fine_far
    e1, e2, e4 = Band(e1m, e1x, C1, C1), Band(e2m, e2x, C1, C1), Band(e4m, e4x, C2, C2)
    t3, t4 = Band(t3m, t3x, C2, C2), Band(t4m, t4x, C2, C2)
    t5, t6 = Band(t5m, t5x, C1, C1), Band(t6m, t6x, C1, C1)
    loads = [pltpu.make_async_copy(b2, whole.at[edges.me, pl.ds(0, 27)], local.at[0])]
    loads += [pltpu.make_async_copy(vol.at[:, h], raw.at[h + 1], local.at[1 + h]) for h in range(H)]
    weights = [pltpu.make_async_copy(x, y, local.at[1 + H + at]) for at, (x, y) in enumerate(zip(given, held))]
    for load in weights[:1] + loads + weights[1:]:
        load.start()
    weights[0].wait()
    for t in range(each):
        taps = [b1[q * each + t] if q * each + t < 27 else jnp.zeros(b1.shape[1:], bf16) for q in range(side)]
        whole[edges.me, 27 + t] = jnp.concatenate(taps, axis=-1)
    edges.greet(gather.partners(), 3)
    start(vol_halo)
    loads[0].wait()
    gather.sideways()
    gather.spread((0, 0))
    turn = one_hot(iota((R, R), 1) == iota((R, R), 0) % C1 * Z + iota((R, R), 0) // C1)

    def settle(row):
        flat = raw[row].astype(f32).reshape(R, W).astype(bf16)
        b_vol[row * R : (row + 1) * R, :] = dot(turn, flat).astype(bf16)

    for h in range(H):
        loads[1 + h].wait()
        settle(h + 1)
    for load in weights[1:]:
        load.wait()
    e1.build(k1, C1, [0])
    block_rows(e1, [b_vol], b_one, R, 1, 1, H - 2, 1)
    e2.build(k2, C1, [0])
    band_kernel(e3, k3, C2, C1, C1, 0, Z // 2, True)
    arrive(vol_halo)
    settle(0)
    settle(H + 1)
    block_row(e1, [b_vol], R, 0, b_one, 1)
    one_halo[0].start()
    block_row(e1, [b_vol], R, H - 1, b_one, H)
    one_halo[1].start()
    gather.receive(part)
    block_rows(e2, [b_one], b_fine, R, 1, 1, H - 2, 2)
    e4.build(k4, C2, [0])
    t3.build(mm, 2 * C2, [0, C2])
    gather.receive(part)
    arrive(one_halo)
    parts = halves(W)
    for h in range(H2):
        block_row(e2, [b_one], R, h * (H - 1), b_fine, h * (H - 1) + 2)
        first, second = b_fine[(2 * h + 2) * R : (2 * h + 3) * R, :], b_fine[(2 * h + 3) * R : (2 * h + 4) * R, :]
        b_pool[(h + 2) * RQ : (h + 3) * RQ, :] = pool(first, second, C1, parts)
        start(pool_halo[2 * h : 2 * h + 2])
    gather.receive(part)
    t4.build(mr, C2, [0])
    t5.build(fm, 2 * C1, [0, C1])
    t6.build(fr, C1, [0])
    gather.receive(shares - 3 * part)
    arrive(pool_halo)
    start(fine_near)
    conv_rows([(e3, b_pool, RQ)], b_first, R2, 0, 1, H2 + 2, 0)
    gather.trade(0, shares // 2)
    edges.blank(b_first, R2, 0, -1)
    edges.blank(b_first, R2, H2 + 1, 1)
    block_rows(e4, [b_first], b_mid, R2, 0, 1, H2, 2)
    first, second = b_mid[2 * R2 : 3 * R2, :], b_mid[3 * R2 : 4 * R2, :]
    b_low[3 * RP : 4 * RP, :] = pool(first, second, C2, halves(W // 2))
    start(low_halo)
    start(mid_halo)
    gather.trade(shares // 2, shares)
    gather.finish()
    wide = Z // 4 * C2
    shape = (C3, side * wide)
    picks = one_hot(iota(shape, 0) == iota(shape, 1) // wide * C2 + (iota(shape, 1) & (C2 - 1)))
    for t in range(each):
        taps = dot(whole[:, 27 + t].reshape(C3, C3), picks).astype(bf16)
        for q in range(side):
            if q * each + t < 27:
                at = (q * each + t) * C3
                kt[at : at + C3, :] = taps[:, q * wide : (q + 1) * wide]

    def tap(a, b, c):
        at = ((a * 3 + b) * 3 + c) * C3
        return kt[at : at + C3, :].astype(f32)

    band(t1, tap, C3, C2, Z // 4)
    for a in range(3):
        for c in range(3):
            for z in range(Z // 4):
                for y in range(Z // 4):
                    r, l = (c * (Z // 4) + z) * C3, (a * (Z // 4) + y) * C3
                    if -1 <= y - z <= 1:
                        t2[r : r + C3, l : l + C3] = whole[:, (a * 3 + y - z + 1) * 3 + c].reshape(C3, C3)
                    else:
                        t2[r : r + C3, l : l + C3] = jnp.zeros((C3, C3), bf16)
    arrive(low_halo)
    narrow = W // 4

    def bottom(banded, source, cells, target, number):
        rows = jnp.concatenate([source[at * cells : (at + 3) * cells, :] for at in range(number)], axis=1)
        for z in range(Z // 4):
            sums = [dot(banded[(c * (Z // 4) + z) * C3 : (c * (Z // 4) + z + 1) * C3, :], rows) for c in range(3)]
            done = finish(jnp.concatenate(sums, axis=0), C3, narrow)
            for at in range(number):
                target[at * RB + z * C3 : at * RB + (z + 1) * C3, :] = done[:, at * narrow : (at + 1) * narrow]

    bottom(t1, b_low, RP, b_bot, 5)
    start(fine_far)
    for step in (-2, -1, 1, 2):
        edges.blank(b_bot, RB, 2 + step, step)
    bottom(t2, b_bot, RB, bot, 3)
    for step in (-1, 1):
        edges.blank(bot, RB, 1 + step, step)
    woven = weave(W // 2)
    for h in range(3):

        def store(a, value):
            at = (2 * h + a) * R2
            b_lift[at : at + R2, :] = value

        lift(bot[h * RB : (h + 1) * RB, :], ub, C3, C2, woven, store)
    arrive(mid_halo)
    block_rows(t3, [b_mid, b_lift], b_three, R2, 0, 1, H2 + 2, 0)
    edges.blank(b_three, R2, 0, -1)
    edges.blank(b_three, R2, H2 + 1, 1)
    for h in range(H2):
        block_row(t4, [b_three], R2, h, four, h + 1)
        if h == 0:
            four_halo[0].start()
    four_halo[1].start()
    woven = weave(W)

    def raise_row(h, which=(0, 1)):
        def store(a, value):
            at = (2 * h + a) * R
            b_raise[at : at + R, :] = value

        lift(four[h * R2 : (h + 1) * R2, :], um, C2, C1, woven, store, which)

    for h in range(1, H2 + 1):
        raise_row(h)
    sources = [b_fine, b_raise]
    block_rows(t5, sources, b_last, R, 2, 1, H - 2, 0)
    arrive(four_halo)
    arrive(fine_near + fine_far)
    raise_row(0)
    raise_row(H2 + 1)
    block_rows(t5, sources, b_last, R, 0, 1, 2, 0)
    block_rows(t5, sources, b_last, R, H, 1, 2, 0)
    edges.blank(b_last, R, 0, -1)
    edges.blank(b_last, R, H + 1, 1)
    saves = []
    for h in range(H):
        block_row(t6, [b_last], R, h, b_vol, h)
        saves.append(pltpu.make_async_copy(b_vol.at[pl.ds(h * R, R)], out.at[pl.ds(h * R, R)], local.at[1 + h]))
        saves[-1].start()
    for save in saves:
        save.wait()
    for halo in edges.halos:
        halo.sent()
    gather.sent()


def per_device(count, *args):
    (volume, f1, f2, m1, m2, b1, b2, ub, mm, mr, um, fm, fr) = args
    C1, H, Z, W = volume.shape
    C2, C3 = m1.shape[3], b2.shape[4]
    own = b1.shape[3]
    R, R2, RP, RL, RB = Z * C1, Z // 2 * C2, Z // 2 * C1, Z // 4 * C2, Z // 4 * C3
    H2, W2, W4 = H // 2, W // 2, W // 4
    flat = lambda k: k.reshape(-1, k.shape[-1])
    each = -(-27 // (C3 // C2))
    taps = 27 + each + (27 + each) % 2
    high = count // 4
    hbm = pl.BlockSpec(memory_space=pl.ANY)
    operands = [
        volume, b2.reshape(27, own, C3), b1.reshape(27, own, C2), flat(f1), flat(f2), flat(m1.swapaxes(3, 4)), flat(m2),
        flat(ub), flat(mm), flat(mr), flat(um), flat(fm), flat(fr),
    ]
    V = lambda *shape: pltpu.VMEM(shape, bf16)
    B = lambda ins, number: (V(384, 384 * number), V(768, 3 * ins * number))
    D = pltpu.SemaphoreType.DMA
    assert H == 4 and Z * C1 == 256 and Z // 2 * C2 == 256
    out = pl.pallas_call(
        functools.partial(network, (H, Z, W, C1, C2, C3), "groups", "rows", count),
        out_shape=jax.ShapeDtypeStruct((H * R, W), bf16),
        in_specs=[hbm] * 13,
        out_specs=hbm,
        scratch_shapes=[V(*x.shape) for x in operands[2:]] + [
            V((H + 2) * R, W), V((H + 2) * R, W), V((H2 + 4) * RP, W2), V((H2 + 2) * R2, W2),
            *B(C1, 1), *B(C1, 1), V(3 * R2, 3 * RP), *B(C2, 1),
            V((H + 4) * R, W), V((H2 + 4) * R2, W2), V(7 * RL, W4), V(5 * RB, W4), V(3 * RB, W4),
            V((H2 + 4) * R2, W2), V((H2 + 2) * R2, W2), V((H2 + 2) * R2, W2), V((H + 4) * R, W), V((H + 2) * R, W),
            V(27 * C3, Z // 4 * C2), V(3 * RB, 3 * RL), V(3 * RB, 3 * RB), *B(C2, 2),
            *B(C2, 1), *B(C1, 2), *B(C1, 1), V(count, taps, own, C3),
            D((22,)), D((22,)), D((2, high)), D((2, high)), D((2, high)), D((2, high)), D((2, 2, high)), D((2, 2, high)),
            V(H + 2, C1, Z, W), D((1 + H + 11,)),
        ],
        compiler_params=pltpu.CompilerParams(collective_id=0, has_side_effects=True, vmem_limit_bytes=VMEM_LIMIT),
        name="network",
    )(*operands)
    return out.reshape(H, Z, C1, W).transpose(2, 0, 1, 3)


def solution(mesh):
    placed = [P(None, ("groups", "rows"), None, None)] + [P()] * 12
    placed[5] = placed[6] = P(None, None, None, "rows", None)
    return jax.shard_map(
        functools.partial(per_device, mesh.shape["rows"]),
        mesh=mesh,
        in_specs=tuple(placed),
        out_specs=P(None, ("groups", "rows"), None, None),
        check_vma=False,
    )
```
